128 devices in a mesh: ctx: 16 (over z, x_lo, core), tp: 8 (over x_hi, y).
Axes of the slice: x: 4 (x_hi: 2, x_lo: 2; x = x_hi * 2 + x_lo), y: 4, z: 4, core: 2. Of those that a mesh axis runs over, the one named last changes fastest.
Arguments:
- hidden_in: bfloat16 [16384, 5376], P(('ctx', 'tp')), may hold values from -6 to 6
- in_gain: float32 [5376], replicated, may hold values from 0.1 to 1.9
- query_weight: bfloat16 [5376, 4096], P('ctx', 'tp'), may hold values from -0.078125 to 0.078125
- key_weight: bfloat16 [5376, 2048], P('ctx', 'tp'), may hold values from -0.078125 to 0.078125
- value_weight: bfloat16 [5376, 2048], P('ctx', 'tp'), may hold values from -0.078125 to 0.078125
- out_weight: bfloat16 [4096, 5376], P('tp', 'ctx'), may hold values from -0.09375 to 0.09375
- q_gain: float32 [128], replicated, may hold values from 0.5 to 16
- k_gain: float32 [128], replicated, may hold values from 0.5 to 16
- post_gain: float32 [5376], replicated, may hold values from 0.1 to 1.9
Outputs:
- layer_out: bfloat16 [16384, 5376], P(('ctx', 'tp'))
The draws below stay inside these ranges and needn't reach their ends.
All inputs are finite; a program needn't handle non-finite values.
Results may differ from the reference program's by a relative error of at most 0.015.
The reference program's roundings to bfloat16 on the way (of `normed`, `queries`, `keys`, `values`, `weights` and `attended`) count: a program that leaves them out, or rounds other values in their place, can miss the bound.
Values may be sent and summed in bfloat16 or wider, within the bound.
A program may use at most 192 MiB of HBM per device.

```python
import math
import jax
import jax.numpy as jnp
from jax import lax

D = 5376
HEADS = 32
KV_HEADS = 16
HEAD_DIM = 128
WINDOW = 1024
TOK_CTX = 1024
SEQ = 16384
SCALAR = 168
N_TP = 8


def gain_law(key):
    return jnp.exp(jax.random.uniform(key, (HEAD_DIM,), jnp.float32, math.log(0.5), math.log(4.0)))


def draw_q_gain(key, part):
    return gain_law(jax.random.fold_in(key, 11))


def draw_k_gain(key, part):
    return gain_law(jax.random.fold_in(key, 23))


def level_of(key, shape, shards, least, top_value):
    level, own = 1.0, jax.random.fold_in(key, 6)
    for axis_at, shards_of in shards:
        draws = jnp.exp(jax.random.uniform(jax.random.fold_in(own, axis_at), (shards_of,), jnp.float32, least / len(shards), top_value / len(shards)))
        level = level * jnp.repeat(draws, shape[axis_at] // shards_of).reshape([-1 if axis == axis_at else 1 for axis in range(len(shape))])
    return level


def bell_draw(own_key, dims, deviation, most, shards=(), held_as=jnp.bfloat16):
    array = deviation * jax.random.normal(own_key, dims, jnp.float32)
    if shards:
        array = array * level_of(own_key, dims, shards, -0.22, 0.18)
    return jnp.clip(array, -most, most).astype(held_as)


def setup_inputs(seed: int = 0) -> dict:
    key_list = jax.random.split(jax.random.key(seed), 10)
    return {
        "hidden_in": bell_draw(key_list[0], (SEQ, D), 1.0, 6.0, ((0, 128),)),
        "in_gain": jnp.clip(1.0 + 0.18 * jax.random.normal(key_list[1], (D,), jnp.float32), 0.1, 1.9),
        "query_weight": bell_draw(key_list[2], (D, HEADS * HEAD_DIM), D ** -0.5, 0.078125, ((0, 16), (1, 8))),
        "key_weight": bell_draw(key_list[3], (D, KV_HEADS * HEAD_DIM), D ** -0.5, 0.078125, ((0, 16), (1, 8))),
        "value_weight": bell_draw(key_list[4], (D, KV_HEADS * HEAD_DIM), D ** -0.5, 0.078125, ((0, 16), (1, 8))),
        "out_weight": bell_draw(key_list[5], (HEADS * HEAD_DIM, D), (HEADS * HEAD_DIM) ** -0.5, 0.09375, ((0, 8), (1, 16))),
        "q_gain": draw_q_gain(jax.random.fold_in(key_list[9], 71), 0),
        "k_gain": draw_k_gain(jax.random.fold_in(key_list[9], 71), 0),
        "post_gain": jnp.clip(1.0 + 0.18 * jax.random.normal(key_list[8], (D,), jnp.float32), 0.1, 1.9),
    }


def rms_scale(values, gain):
    return values * lax.rsqrt(lax.optimization_barrier(jnp.mean(values * values, axis=-1, keepdims=True)) + 1e-06) * gain

def rotate(vectors, positions):
    half_dim = vectors.shape[-1] // 2
    frequency = 10000.0 ** (-(jnp.arange(half_dim, dtype=jnp.float32) * 2.0 / vectors.shape[-1]))
    angles = positions.astype(jnp.float32)[:, None] * frequency[None, :]
    cosine = jnp.cos(angles)[:, None, :]
    sine_part = jnp.sin(angles)[:, None, :]
    first_half = vectors[..., :half_dim]
    second_half = vectors[..., half_dim:]
    return jnp.concatenate([first_half * cosine - second_half * sine_part, second_half * cosine + first_half * sine_part], axis=-1)

def attend(queries, keys, values, query_pos, key_pos):
    row_count, query_heads, head_dim = queries.shape
    key_heads = keys.shape[1]
    group_size = query_heads // key_heads
    grouped = queries.reshape(row_count, key_heads, group_size, head_dim).astype(jnp.float32)
    scores = jnp.einsum('rhgd,khd->hgrk', grouped, keys.astype(jnp.float32))
    offset = query_pos[:, None] - key_pos[None, :]
    allowed = (offset >= 0) & (offset < WINDOW) & (key_pos[None, :] >= 0)
    scores = jnp.where(allowed, scores * float(SCALAR) ** (-0.5), -1e+30)
    row_max = lax.optimization_barrier(jnp.max(scores, axis=-1, keepdims=True))
    expo = jnp.where(allowed, jnp.exp(scores - row_max), 0.0)
    weights = (expo / lax.optimization_barrier(jnp.sum(expo, axis=-1, keepdims=True))).astype(jnp.bfloat16)
    mixed = jnp.einsum('hgrk,khd->rhgd', weights.astype(jnp.float32), values.astype(jnp.float32))
    return mixed.astype(jnp.bfloat16).reshape(row_count, query_heads * head_dim)

def reference(hidden_in, in_gain, query_weight, key_weight, value_weight, out_weight, q_gain, k_gain, post_gain):
    inputs = hidden_in.astype(jnp.float32)
    normed = rms_scale(inputs, in_gain).astype(jnp.bfloat16)
    positions = jnp.arange(SEQ, dtype=jnp.int32)
    query_raw = jnp.dot(normed, query_weight, preferred_element_type=jnp.float32).reshape(SEQ, HEADS, HEAD_DIM)
    queries = rotate(rms_scale(query_raw, q_gain), positions).astype(jnp.bfloat16)
    key_raw = jnp.dot(normed, key_weight, preferred_element_type=jnp.float32).reshape(SEQ, KV_HEADS, HEAD_DIM)
    keys = rotate(rms_scale(key_raw, k_gain), positions).astype(jnp.bfloat16)
    values = jnp.dot(normed, value_weight, preferred_element_type=jnp.float32).astype(jnp.bfloat16).reshape(SEQ, KV_HEADS, HEAD_DIM)
    padding = jnp.zeros((WINDOW, KV_HEADS, HEAD_DIM), jnp.bfloat16)
    keys_padded = jnp.concatenate([padding, keys], axis=0)
    values_padded = jnp.concatenate([padding, values], axis=0)
    group_cols = HEADS * HEAD_DIM // N_TP
    out_groups = out_weight.reshape(N_TP, group_cols, D).astype(jnp.float32)

    def one_block(block_id):
        first_row = (block_id * TOK_CTX).astype(jnp.int32)
        block_queries = lax.dynamic_slice_in_dim(queries, first_row, TOK_CTX, 0)
        block_keys = lax.dynamic_slice_in_dim(keys_padded, first_row, TOK_CTX + WINDOW, 0)
        block_values = lax.dynamic_slice_in_dim(values_padded, first_row, TOK_CTX + WINDOW, 0)
        query_pos = first_row + jnp.arange(TOK_CTX, dtype=jnp.int32)
        key_pos = first_row - WINDOW + jnp.arange(TOK_CTX + WINDOW, dtype=jnp.int32)
        attended = attend(block_queries, block_keys, block_values, query_pos, key_pos)
        split_heads = attended.reshape(TOK_CTX, N_TP, group_cols).astype(jnp.float32)
        partial_value = jnp.einsum('rtc,tcd->trd', split_heads, out_groups).astype(jnp.bfloat16)
        partial_value = lax.optimization_barrier(partial_value)
        projected = lax.optimization_barrier(jnp.sum(partial_value.astype(jnp.float32), axis=0))
        block_in = lax.dynamic_slice_in_dim(inputs, first_row, TOK_CTX, 0)
        return (block_in + rms_scale(projected, post_gain)).astype(jnp.bfloat16)
    blocks = lax.map(one_block, jnp.arange(SEQ // TOK_CTX, dtype=jnp.int32))
    return blocks.reshape(SEQ, D)
```

```python
import functools

import jax
import jax.numpy as jnp
from jax import lax
from jax.experimental import pallas as pl
from jax.experimental.pallas import tpu as pltpu
from jax.sharding import PartitionSpec as P

WINDOW = 1024
SCALE = 168.0 ** (-0.5)
EPS = 1e-06
D = 5376
PIECE = 336
TOK = 512
HEAD = 128
KCH = 768
NK = D // KCH
TILE = 896
NT = D // TILE
MESH = pl.DeviceIdType.MESH
BF = jnp.bfloat16
F32 = jnp.float32

STEP_A = (-1, 1, 0, 0, 2, -1, -1, 1, 1, 0, -1, 2, 2, 1, 2)
STEP_B = (0, 0, -1, 1, 0, -1, 1, -1, 1, 2, 2, -1, 1, 2, 2)
NSTEP = 15


def pick(k, values):
    out = jnp.int32(values[-1])
    for i in range(len(values) - 2, -1, -1):
        if values[i] != values[-1]:
            out = jnp.where(k == i, jnp.int32(values[i]), out)
    return out


def among(k, values):
    hit = k == values[0]
    for v in values[1:]:
        hit = hit | (k == v)
    return hit


def kernel(
    hid_ref, ing_ref, wq_ref, wk_ref, wv_ref, wo_ref, cos_ref, sin_ref, qg_ref, kg_ref, pg_ref,
    out_ref,
    w, act, kv, q, att, acc, bias, relay, rbuf, proj,
    own_sem, ici_recv, part_recv, ici_send, part_send,
    act_recv, act_send, halo_recv, halo_send, relay_recv, rs_recv, rs_send,
):
    ctx = lax.axis_index("ctx")
    tp = lax.axis_index("tp")
    z, xl, c = ctx // 4, (ctx // 2) % 2, ctx % 2
    xh, y = tp // 4, tp % 4
    x = xh * 2 + xl
    block = (z * 2 + xl) * 4 + c * 2 + xh

    def dev(dx, dz, core, dy):
        xx, zz, yy = (x + dx + 4) % 4, (z + dz + 4) % 4, (y + dy + 4) % 4
        return (zz * 4 + (xx % 2) * 2 + core, (xx // 2) * 4 + yy)

    def block_dev(b):
        return ((b // 8) * 4 + ((b // 4) % 2) * 2 + (b // 2) % 2, (b % 2) * 4 + y)

    yp, ym = dev(0, 0, c, 1), dev(0, 0, c, -1)
    partner = dev(0, 0, 1 - c, 0)
    ahead = [block_dev((block + 1) % 32), block_dev((block + 2) % 32)]
    behind = [block_dev((block + 31) % 32), block_dev((block + 30) % 32)]

    barrier = pltpu.get_barrier_semaphore()
    peers = [dev(1, 0, c, 0), dev(-1, 0, c, 0), dev(0, 1, c, 0), dev(0, -1, c, 0), yp, ym, partner]
    peers += ahead + behind
    for peer in peers:
        pl.semaphore_signal(barrier, inc=1, device_id=peer, device_id_type=MESH)

    own_rows = pl.ds(pl.multiple_of(ctx * PIECE, 16), PIECE)
    loads = [
        pltpu.make_async_copy(wk_ref, w.at[0, xh, own_rows, pl.ds(0, 256)], own_sem.at[0]),
        pltpu.make_async_copy(wv_ref, w.at[0, xh, own_rows, pl.ds(256, 256)], own_sem.at[1]),
        pltpu.make_async_copy(wq_ref, w.at[1, xh, own_rows], own_sem.at[2]),
        pltpu.make_async_copy(wo_ref, w.at[2, xh, own_rows], own_sem.at[3]),
    ]
    for load in loads:
        load.start()

    def x_first(s):
        return c == 0

    def axis_dev(s, first, sign):
        along_x = x_first(s) if first else jnp.logical_not(x_first(s))
        dx = jnp.where(along_x, sign, 0)
        dz = jnp.where(along_x, 0, sign)
        return dev(dx, dz, c, 0)

    def piece(s, da, db):
        fx = x_first(s)
        dx, dz = jnp.where(fx, da, db), jnp.where(fx, db, da)
        xx, zz = (x + dx + 4) % 4, (z + dz + 4) % 4
        row = pl.multiple_of((zz * 4 + (xx % 2) * 2 + c) * PIECE, 16)
        return w.at[s, xx // 2, pl.ds(row, PIECE)]

    def send(s, ref, device, at):
        pltpu.make_async_remote_copy(
            src_ref=ref, dst_ref=ref, send_sem=ici_send.at[s], recv_sem=ici_recv.at[s, at],
            device_id=device, device_id_type=MESH,
        ).start()

    def send_partner(s, ref):
        pltpu.make_async_remote_copy(
            src_ref=ref, dst_ref=ref, send_sem=part_send.at[s], recv_sem=part_recv.at[s],
            device_id=partner, device_id_type=MESH,
        ).start()

    def start_own(s):
        ref = piece(s, 0, 0)
        send(s, ref, axis_dev(s, True, 1), 0)
        send(s, ref, axis_dev(s, True, -1), 1)
        send(s, ref, axis_dev(s, False, 1), 2)
        send(s, ref, axis_dev(s, False, -1), 3)
        send_partner(s, ref)

    def comm_step(g):
        s, k = g // NSTEP, g % NSTEP
        ref = piece(s, pick(k, STEP_A), pick(k, STEP_B))
        pltpu.make_async_copy(ref, ref, ici_recv.at[s, k]).wait()

        @pl.when(among(k, (0, 1, 4, 2, 7)))
        def _():
            send(s, ref, axis_dev(s, False, 1), pick(k, (5, 7, 9, 0, 11, 0, 0, 13)))

        @pl.when(among(k, (0, 1, 4, 6, 12)))
        def _():
            send(s, ref, axis_dev(s, False, -1), pick(k, (6, 8, 0, 0, 12, 0, 10, 0, 0, 0, 0, 0, 14)))

        @pl.when((k == 0) & (s % 2 == 0))
        def _():
            send(s, ref, axis_dev(s, True, 1), 4)

        @pl.when((k == 1) & (s % 2 == 1))
        def _():
            send(s, ref, axis_dev(s, True, -1), 4)

        send_partner(s, ref)

        @pl.when((k == 8) & (s < 2))
        def _():
            start_own(s + 1)

    def await_partner(s):
        pltpu.make_async_copy(w.at[s, 0], w.at[s, 0], part_recv.at[s]).wait()

    pl.semaphore_wait(barrier, len(peers))
    loads[0].wait()
    loads[1].wait()
    start_own(0)

    hid = hid_ref[...].astype(F32)
    mean = jnp.mean(hid * hid, axis=-1, keepdims=True)
    act[y] = (hid * lax.rsqrt(mean + EPS) * ing_ref[...]).astype(BF)
    loads[2].wait()
    loads[3].wait()

    def act_copy(owner, half, device, at):
        ref = act.at[owner, pl.ds(half * 64, 64)]
        return pltpu.make_async_remote_copy(
            src_ref=ref, dst_ref=ref, send_sem=act_send, recv_sem=act_recv.at[at],
            device_id=device, device_id_type=MESH,
        )

    act_copy(y, 0, yp, 0).start()
    act_copy(y, 1, ym, 3).start()
    act_copy(y, 1, yp, 1).start()
    act_copy(y, 0, ym, 2).start()
    before, after, across = (y + 3) % 4, (y + 1) % 4, (y + 2) % 4

    row = lax.broadcasted_iota(jnp.int32, (HEAD, 1152), 0)
    col = lax.broadcasted_iota(jnp.int32, (HEAD, 1152), 1)

    def mask_body(qc, carry):
        least = WINDOW - block * TOK - qc * 128
        allowed = (col > row) & (col <= row + WINDOW) & (col >= least)
        bias[qc] = jnp.where(allowed, 0.0, -1e30)
        return carry

    lax.fori_loop(0, 4, mask_body, 0)

    def stream_body(g, carry):
        comm_step(g)

        @pl.when(g == 8)
        def _():
            act_copy(before, 0, yp, 0).wait_recv()
            act_copy(before, 0, yp, 4).start()
            act_copy(after, 1, ym, 3).wait_recv()
            act_copy(after, 1, ym, 5).start()

        return carry

    lax.fori_loop(0, 22, stream_body, 0)
    act_copy(before, 1, yp, 1).wait_recv()
    act_copy(after, 0, ym, 2).wait_recv()
    act_copy(across, 0, yp, 4).wait_recv()
    act_copy(across, 1, ym, 5).wait_recv()
    await_partner(0)

    def project(s, j):
        half, kk = j // NK, j % NK
        left = act[:, :, pl.ds(pl.multiple_of(kk * KCH, KCH), KCH)].reshape(TOK, KCH)
        right = w[s, half, pl.ds(pl.multiple_of(kk * KCH, KCH), KCH), :]
        part = jnp.dot(left, right, preferred_element_type=F32)

        @pl.when(kk == 0)
        def _():
            acc[...] = part

        @pl.when(kk > 0)
        def _():
            acc[...] += part

    def normed_rope(vec, gain):
        mean = jnp.mean(vec * vec, axis=-1, keepdims=True)
        vec = vec * lax.rsqrt(mean + EPS) * gain
        return (vec * cos_ref[...] + pltpu.roll(vec, HEAD // 2, 1) * sin_ref[...]).astype(BF)

    def halo_copy(half, ahead_by):
        heads = pl.ds(half * 2, 2)
        return pltpu.make_async_remote_copy(
            src_ref=kv.at[:, heads, pl.ds(2 * TOK, TOK)],
            dst_ref=kv.at[:, heads, pl.ds((2 - ahead_by) * TOK, TOK)],
            send_sem=halo_send, recv_sem=halo_recv.at[ahead_by - 1, half],
            device_id=ahead[ahead_by - 1], device_id_type=MESH,
        )

    def kv_chunk(j):
        project(0, j)
        half = j // NK

        @pl.when(j % NK == NK - 1)
        def _():
            for h in range(2):
                kv[0, half * 2 + h, pl.ds(2 * TOK, TOK)] = normed_rope(
                    acc[:, h * HEAD : (h + 1) * HEAD], kg_ref[...]
                )
                kv[1, half * 2 + h, pl.ds(2 * TOK, TOK)] = acc[
                    :, (2 + h) * HEAD : (3 + h) * HEAD
                ].astype(BF)
            halo_copy(half, 1).start()
            halo_copy(half, 2).start()

    def q_chunk(j):
        project(1, j)
        half = j // NK

        @pl.when(j % NK == NK - 1)
        def _():
            for h in range(4):
                q[half * 2 + h // 2, h % 2] = normed_rope(
                    acc[:, h * HEAD : (h + 1) * HEAD], qg_ref[...]
                )

    def kv_body(j, carry):
        kv_chunk(j)

        @pl.when(j % 2 == 1)
        def _():
            comm_step(22 + j // 2)

        return carry

    lax.fori_loop(0, 2 * NK, kv_body, 0)
    comm_step(29)
    await_partner(1)

    def q_body(j, carry):
        q_chunk(j)

        @pl.when(j % 2 == 1)
        def _():
            comm_step(30 + j // 2)

        return carry

    lax.fori_loop(0, 2 * NK, q_body, 0)
    for half in range(2):
        halo_copy(half, 1).wait_recv()
        halo_copy(half, 2).wait_recv()

    def attend_body(it, carry):
        qc, kvh = it // 4, it % 4
        start = pl.multiple_of(qc * 128, 128)
        queries = q[kvh, :, pl.ds(start, 128), :].reshape(256, HEAD)
        keys = kv[0, kvh, pl.ds(start, 1152), :]
        values = kv[1, kvh, pl.ds(start, 1152), :]
        scores = lax.dot_general(
            queries, keys, (((1,), (1,)), ((), ())), preferred_element_type=F32
        )
        scores = scores.reshape(2, 128, 1152) * SCALE + bias[qc][None]
        expo = jnp.exp(scores - jnp.max(scores, axis=-1, keepdims=True))
        weights = (expo * (1.0 / jnp.sum(expo, axis=-1, keepdims=True))).astype(BF)
        mixed = jnp.dot(weights.reshape(256, 1152), values, preferred_element_type=F32).astype(BF)
        for h in range(2):
            lanes = pl.ds(pl.multiple_of((kvh % 2) * 256 + h * 128, 128), 128)
            att[kvh // 2, pl.ds(start, 128), lanes] = mixed[h * 128 : (h + 1) * 128]

        @pl.when(it % 2 == 1)
        def _():
            comm_step(37 + it // 2)

        return carry

    lax.fori_loop(0, 16, attend_body, 0)
    await_partner(2)
    pltpu.make_async_copy(act.at[pl.ds(0, 3)], act.at[pl.ds(0, 3)], act_send).wait()

    def lanes_of(n):
        return pl.ds(pl.multiple_of(n * TILE, 128), TILE)

    def relay_copy(n, device):
        return pltpu.make_async_remote_copy(
            src_ref=act.at[across, :, lanes_of(n)], dst_ref=relay.at[:, lanes_of(n)],
            send_sem=rs_send, recv_sem=relay_recv.at[n], device_id=device, device_id_type=MESH,
        )

    def sum_copy(n, chunk, side, device):
        return pltpu.make_async_remote_copy(
            src_ref=act.at[chunk, :, lanes_of(n)], dst_ref=rbuf.at[side, :, lanes_of(n)],
            send_sem=rs_send, recv_sem=rs_recv.at[side, n], device_id=device, device_id_type=MESH,
        )

    def out_body(n, carry):
        @pl.when(n < NT)
        def _():
            rows = pl.ds(pl.multiple_of(n * TILE, 128), TILE)
            part = lax.dot_general(
                att[0], w[2, 0, rows, :], (((1,), (1,)), ((), ())), preferred_element_type=F32
            )
            part += lax.dot_general(
                att[1], w[2, 1, rows, :], (((1,), (1,)), ((), ())), preferred_element_type=F32
            )
            act[:, :, lanes_of(n)] = part.astype(BF).reshape(4, 128, TILE)

            @pl.when(n % 2 == 0)
            def _():
                relay_copy(n, yp).start()
                sum_copy(n, before, 1, ym).start()

            @pl.when(n % 2 == 1)
            def _():
                relay_copy(n, ym).start()
                sum_copy(n, after, 0, yp).start()

        @pl.when(n > 0)
        def _():
            m = n - 1
            relay_copy(m, yp).wait_recv()
            chunk = jnp.where(m % 2 == 0, after, before)
            merged = act[chunk, :, lanes_of(m)].astype(F32) + relay[:, lanes_of(m)].astype(F32)
            act[chunk, :, lanes_of(m)] = merged.astype(BF)

            @pl.when(m % 2 == 0)
            def _():
                sum_copy(m, after, 0, yp).start()

            @pl.when(m % 2 == 1)
            def _():
                sum_copy(m, before, 1, ym).start()

        return carry

    lax.fori_loop(0, NT + 1, out_body, 0)

    def sum_body(n, total):
        sum_copy(n, after, 0, yp).wait_recv()
        sum_copy(n, before, 1, ym).wait_recv()
        value = (
            act[y, :, lanes_of(n)].astype(F32)
            + rbuf[0, :, lanes_of(n)].astype(F32)
            + rbuf[1, :, lanes_of(n)].astype(F32)
        )
        proj[:, lanes_of(n)] = value
        return total + jnp.sum(value * value, axis=-1, keepdims=True)

    total = lax.fori_loop(0, NT, sum_body, jnp.zeros((128, 1), F32))
    scale = lax.rsqrt(total * (1.0 / D) + EPS)
    out_ref[...] = (hid_ref[...].astype(F32) + proj[...] * scale * pg_ref[...]).astype(BF)

    for s in range(3):
        sent = w.at[s, 0, pl.ds(0, NSTEP * PIECE)]
        pltpu.make_async_copy(sent, sent, ici_send.at[s]).wait()
        pltpu.make_async_copy(w.at[s, 0], w.at[s, 0], part_send.at[s]).wait()
    halo = kv.at[:, :, pl.ds(0, 2 * TOK)]
    pltpu.make_async_copy(halo, halo, halo_send).wait()
    pltpu.make_async_copy(act.at[pl.ds(0, 3)], act.at[pl.ds(0, 3)], rs_send).wait()


def per_device(
    hidden_in, in_gain, query_weight, key_weight, value_weight, out_weight, q_gain, k_gain, post_gain
):
    ctx, tp = lax.axis_index("ctx"), lax.axis_index("tp")
    block = ctx * 2 + tp // 4
    positions = block * TOK + jnp.arange(TOK, dtype=jnp.int32)
    frequency = 10000.0 ** (-(jnp.arange(HEAD // 2, dtype=F32) * 2.0 / HEAD))
    angles = positions.astype(F32)[:, None] * frequency[None, :]
    cosine, sine = jnp.cos(angles), jnp.sin(angles)
    cos_table = jnp.concatenate([cosine, cosine], axis=-1)
    sin_table = jnp.concatenate([-sine, sine], axis=-1)
    vmem, hbm = pl.BlockSpec(memory_space=pltpu.VMEM), pl.BlockSpec(memory_space=pl.ANY)
    dma = pltpu.SemaphoreType.DMA
    return pl.pallas_call(
        kernel,
        out_shape=jax.ShapeDtypeStruct((128, D), BF),
        in_specs=[vmem, vmem, hbm, hbm, hbm, hbm, vmem, vmem, vmem, vmem, vmem],
        out_specs=vmem,
        scratch_shapes=[
            pltpu.VMEM((3, 2, D, 512), BF),
            pltpu.VMEM((4, 128, D), BF),
            pltpu.VMEM((2, 4, 3 * TOK, HEAD), BF),
            pltpu.VMEM((4, 2, TOK, HEAD), BF),
            pltpu.VMEM((2, TOK, 512), BF),
            pltpu.VMEM((TOK, 512), F32),
            pltpu.VMEM((4, 128, 1152), F32),
            pltpu.VMEM((128, D), BF),
            pltpu.VMEM((2, 128, D), BF),
            pltpu.VMEM((128, D), F32),
            dma((4,)), dma((3, NSTEP)), dma((3,)), dma((3,)), dma((3,)),
            dma((6,)), dma, dma((2, 2)), dma, dma((NT,)), dma((2, NT)), dma,
        ],
        compiler_params=pltpu.CompilerParams(
            collective_id=0, has_side_effects=True, vmem_limit_bytes=67043328
        ),
    )(
        hidden_in,
        in_gain.reshape(1, D),
        query_weight,
        key_weight,
        value_weight,
        out_weight.T,
        cos_table,
        sin_table,
        q_gain.reshape(1, HEAD),
        k_gain.reshape(1, HEAD),
        post_gain.reshape(1, D),
    )


def solution(mesh):
    in_specs = (
        P(("ctx", "tp"), None), P(), P("ctx", "tp"), P("ctx", "tp"), P("ctx", "tp"), P("tp", "ctx"),
        P(), P(), P(),
    )
    return jax.shard_map(
        per_device, mesh=mesh, in_specs=in_specs, out_specs=P(("ctx", "tp"), None), check_vma=False
    )
```

```python
import functools

import jax
import jax.numpy as jnp
from jax import lax
from jax.experimental import pallas as pl
from jax.experimental.pallas import tpu as pltpu
from jax.sharding import PartitionSpec as P

WINDOW = 1024
SCALE = 168.0 ** (-0.5)
EPS = 1e-06
D = 5376
PIECE = 336
TOK = 512
HEAD = 128
KCH = 768
NK = D // KCH
NT = 16
LAG = 2
MESH = pl.DeviceIdType.MESH
BF = jnp.bfloat16
F32 = jnp.float32

STEP_A = (-1, 1, 0, 0, 2, -1, -1, 1, 1, 0, -1, 2, 2, 1, 2)
STEP_B = (0, 0, -1, 1, 0, -1, 1, -1, 1, 2, 2, -1, 1, 2, 2)
NSTEP = 15
Q_ORDER = (0, 2, 6, 1, 4, 3, 5, 2, 0, 4, 1, 3, 6, 5, 4, 2, 6, 3, 5, 0, 1, 6, 4, 0, 5, 2, 1, 3)
LOG2E = 1.4426950408889634


def pick(k, values):
    out = jnp.int32(values[-1])
    for i in range(len(values) - 2, -1, -1):
        if values[i] != values[-1]:
            out = jnp.where(k == i, jnp.int32(values[i]), out)
    return out


def among(k, values):
    hit = k == values[0]
    for v in values[1:]:
        hit = hit | (k == v)
    return hit


def kernel(
    hid_ref, ing_ref, wq_ref, wk_ref, wv_ref, wo_ref, cos_ref, sin_ref, qg_ref, kg_ref, pg_ref,
    out_ref,
    w, act, kv, q, att, acc, bias, relay, rbuf, proj,
    own_sem, ici_recv, part_recv, ici_send, part_send,
    act_recv, act_send, halo_recv, halo_send, relay_recv, rs_recv, rs_send,
):
    ctx = lax.axis_index("ctx")
    tp = lax.axis_index("tp")
    z, xl, c = ctx // 4, (ctx // 2) % 2, ctx % 2
    xh, y = tp // 4, tp % 4
    x = xh * 2 + xl
    block = (z * 2 + xl) * 4 + c * 2 + xh

    def dev(dx, dz, core, dy):
        xx, zz, yy = (x + dx + 4) % 4, (z + dz + 4) % 4, (y + dy + 4) % 4
        return (zz * 4 + (xx % 2) * 2 + core, (xx // 2) * 4 + yy)

    def block_dev(b):
        return ((b // 8) * 4 + ((b // 4) % 2) * 2 + (b // 2) % 2, (b % 2) * 4 + y)

    yp, ym = dev(0, 0, c, 1), dev(0, 0, c, -1)
    partner = dev(0, 0, 1 - c, 0)
    ahead = [block_dev((block + 1) % 32), block_dev((block + 2) % 32)]
    behind = [block_dev((block + 31) % 32), block_dev((block + 30) % 32)]

    barrier = pltpu.get_barrier_semaphore()
    peers = [dev(1, 0, c, 0), dev(-1, 0, c, 0), dev(0, 1, c, 0), dev(0, -1, c, 0), yp, ym, partner]
    peers += ahead + behind
    for peer in peers:
        pl.semaphore_signal(barrier, inc=1, device_id=peer, device_id_type=MESH)

    own_rows = pl.ds(pl.multiple_of(ctx * PIECE, 16), PIECE)
    loads = [
        pltpu.make_async_copy(wk_ref, w.at[0, xh, own_rows, pl.ds(0, 256)], own_sem.at[0]),
        pltpu.make_async_copy(wv_ref, w.at[0, xh, own_rows, pl.ds(256, 256)], own_sem.at[1]),
        pltpu.make_async_copy(wq_ref, w.at[1, xh, own_rows], own_sem.at[2]),
        pltpu.make_async_copy(wo_ref, w.at[2, xh, own_rows], own_sem.at[3]),
    ]
    for load in loads:
        load.start()

    def x_first(s):
        return (c == 0) | (s == 1)

    def axis_dev(s, first, sign):
        along_x = x_first(s) if first else jnp.logical_not(x_first(s))
        dx = jnp.where(along_x, sign, 0)
        dz = jnp.where(along_x, 0, sign)
        return dev(dx, dz, c, 0)

    def piece(s, da, db):
        fx = x_first(s)
        dx, dz = jnp.where(fx, da, db), jnp.where(fx, db, da)
        xx, zz = (x + dx + 4) % 4, (z + dz + 4) % 4
        row = pl.multiple_of((zz * 4 + (xx % 2) * 2 + c) * PIECE, 16)
        return w.at[s, xx // 2, pl.ds(row, PIECE)]

    def send(s, ref, device, at):
        pltpu.make_async_remote_copy(
            src_ref=ref, dst_ref=ref, send_sem=ici_send.at[s], recv_sem=ici_recv.at[s, at],
            device_id=device, device_id_type=MESH,
        ).start()

    def send_partner(s, ref, k):
        late = jnp.where((s == 1) & (k > 12) & (k < NSTEP), 1, 0)
        pltpu.make_async_remote_copy(
            src_ref=ref, dst_ref=ref, send_sem=part_send.at[s],
            recv_sem=part_recv.at[s, jnp.where(s == 2, k, late)],
            device_id=partner, device_id_type=MESH,
        ).start()

    def start_own(s):
        ref = piece(s, 0, 0)
        send(s, ref, axis_dev(s, True, 1), 0)
        send(s, ref, axis_dev(s, True, -1), 1)
        send(s, ref, axis_dev(s, False, 1), 2)
        send(s, ref, axis_dev(s, False, -1), 3)
        send_partner(s, ref, NSTEP)

    def comm_step(g):
        s, k = g // NSTEP, g % NSTEP
        ref = piece(s, pick(k, STEP_A), pick(k, STEP_B))
        pltpu.make_async_copy(ref, ref, ici_recv.at[s, k]).wait()

        @pl.when(among(k, (0, 1, 4, 2, 7)))
        def _():
            send(s, ref, axis_dev(s, False, 1), pick(k, (5, 7, 9, 0, 11, 0, 0, 13)))

        @pl.when(among(k, (0, 1, 4, 6, 12)))
        def _():
            send(s, ref, axis_dev(s, False, -1), pick(k, (6, 8, 0, 0, 12, 0, 10, 0, 0, 0, 0, 0, 14)))

        @pl.when((k == 0) & (s % 2 == 0))
        def _():
            send(s, ref, axis_dev(s, True, 1), 4)

        @pl.when((k == 1) & (s % 2 == 1))
        def _():
            send(s, ref, axis_dev(s, True, -1), 4)

        send_partner(s, ref, k)

        @pl.when((k == 8) & (s < 2))
        def _():
            start_own(s + 1)

    def await_partner(s, at, count):
        ref = w.at[s, 0, pl.ds(0, count * PIECE)]
        pltpu.make_async_copy(ref, ref, part_recv.at[s, at]).wait()

    pl.semaphore_wait(barrier, len(peers))
    loads[0].wait()
    loads[1].wait()
    start_own(0)

    hid = hid_ref[...].astype(F32)
    mean = jnp.mean(hid * hid, axis=-1, keepdims=True)
    act[y] = (hid * lax.rsqrt(mean + EPS) * ing_ref[...]).astype(BF)
    loads[2].wait()
    loads[3].wait()

    def act_copy(owner, half, device, at):
        ref = act.at[owner, pl.ds(half * 64, 64)]
        return pltpu.make_async_remote_copy(
            src_ref=ref, dst_ref=ref, send_sem=act_send, recv_sem=act_recv.at[at],
            device_id=device, device_id_type=MESH,
        )

    act_copy(y, 0, yp, 0).start()
    act_copy(y, 1, ym, 3).start()
    act_copy(y, 1, yp, 1).start()
    act_copy(y, 0, ym, 2).start()
    before, after, across = (y + 3) % 4, (y + 1) % 4, (y + 2) % 4

    row = lax.broadcasted_iota(jnp.int32, (HEAD, 1152), 0)
    col = lax.broadcasted_iota(jnp.int32, (HEAD, 1152), 1)

    def mask_body(qc, carry):
        least = WINDOW - block * TOK - qc * 128
        allowed = (col > row) & (col <= row + WINDOW) & (col >= least)
        bias[qc] = jnp.where(allowed, 0.0, -1e30)
        return carry

    lax.fori_loop(0, 4, mask_body, 0)

    def stream_body(g, carry):
        comm_step(g)

        @pl.when(g == 8)
        def _():
            act_copy(before, 0, yp, 0).wait_recv()
            act_copy(before, 0, yp, 4).start()
            act_copy(after, 1, ym, 3).wait_recv()
            act_copy(after, 1, ym, 5).start()

        return carry

    lax.fori_loop(0, 19, stream_body, 0)
    act_copy(before, 1, yp, 1).wait_recv()
    act_copy(after, 0, ym, 2).wait_recv()
    act_copy(across, 0, yp, 4).wait_recv()
    act_copy(across, 1, ym, 5).wait_recv()
    await_partner(0, 0, 16)

    def project(s, half, kk, first):
        rows = pl.ds(pl.multiple_of(kk * KCH, KCH), KCH)
        left = act[:, :, rows].reshape(TOK, KCH)
        part = jnp.dot(left, w[s, half, rows, :], preferred_element_type=F32)

        @pl.when(first)
        def _():
            acc[half] = part

        @pl.when(jnp.logical_not(first))
        def _():
            acc[half] += part

    def normed_rope(vec, gain):
        mean = jnp.mean(vec * vec, axis=-1, keepdims=True)
        vec = vec * lax.rsqrt(mean + EPS) * gain
        return (vec * cos_ref[...] + pltpu.roll(vec, HEAD // 2, 1) * sin_ref[...]).astype(BF)

    def halo_copy(half, ahead_by):
        heads = pl.ds(half * 2, 2)
        return pltpu.make_async_remote_copy(
            src_ref=kv.at[:, heads, pl.ds(2 * TOK, TOK)],
            dst_ref=kv.at[:, heads, pl.ds((2 - ahead_by) * TOK, TOK)],
            send_sem=halo_send, recv_sem=halo_recv.at[ahead_by - 1, half],
            device_id=ahead[ahead_by - 1], device_id_type=MESH,
        )

    def kv_body(j, carry):
        half, kk = j // NK, j % NK
        project(0, half, kk, kk == 0)

        @pl.when(kk == NK - 1)
        def _():
            for h in range(2):
                kv[0, half * 2 + h, pl.ds(2 * TOK, TOK)] = normed_rope(
                    acc[half, :, h * HEAD : (h + 1) * HEAD], kg_ref[...]
                )
                kv[1, half * 2 + h, pl.ds(2 * TOK, TOK)] = acc[
                    half, :, (2 + h) * HEAD : (3 + h) * HEAD
                ].astype(BF)
            halo_copy(half, 1).start()
            halo_copy(half, 2).start()

        @pl.when(j % 4 == 3)
        def _():
            comm_step(19 + j // 4)

        return carry

    def step_body(g, carry):
        comm_step(g)
        return carry

    lax.fori_loop(0, 2 * NK, kv_body, 0)
    lax.fori_loop(22, 28, step_body, 0)
    await_partner(1, 0, 14)

    def q_body(j, carry):
        half, p = j % 2, j // 2

        @pl.when(j == 8)
        def _():
            await_partner(1, 1, 2)

        project(1, half, pick(z * NK + p, Q_ORDER), p == 0)

        @pl.when(p == NK - 1)
        def _():
            for h in range(4):
                q[half * 2 + h // 2, h % 2] = normed_rope(
                    acc[half, :, h * HEAD : (h + 1) * HEAD], qg_ref[...]
                )

        @pl.when((j == 3) | (j == 7) | (j == 9) | (j == 11) | (j == 13))
        def _():
            comm_step(pick(j // 2, (0, 28, 0, 29, 30, 31, 32)))

        return carry

    lax.fori_loop(0, 2 * NK, q_body, 0)
    for half in range(2):
        halo_copy(half, 1).wait_recv()
        halo_copy(half, 2).wait_recv()

    def attend(rel, qc, kvh):
        start = pl.multiple_of(qc * 128, 128)
        queries = q[kvh, :, pl.ds(start, 128), :].reshape(256, HEAD)
        keys = kv[0, kvh, pl.ds(start, 1152), :]
        values = kv[1, kvh, pl.ds(start, 1152), :]
        scores = lax.dot_general(
            queries, keys, (((1,), (1,)), ((), ())), preferred_element_type=F32
        )
        scores = scores.reshape(2, 128, 1152) * (SCALE * LOG2E) + bias[qc][None]
        expo = jnp.exp2(scores - jnp.max(scores, axis=-1, keepdims=True))
        weights = (expo * (1.0 / jnp.sum(expo, axis=-1, keepdims=True))).astype(BF)
        mixed = jnp.dot(weights.reshape(256, 1152), values, preferred_element_type=F32).astype(BF)
        rows = pl.ds(pl.multiple_of(rel * 128, 128), 128)
        for h in range(2):
            lanes = pl.ds(pl.multiple_of((kvh % 2) * 256 + h * 128, 128), 128)
            att[kvh // 2, rows, lanes] = mixed[h * 128 : (h + 1) * 128]

    def attend_body(it, carry):
        rel, pair = it // 2, it % 2
        qc = (y + pick(rel, (2, 1, 3, 0))) % 4
        attend(rel, qc, pair * 2)
        attend(rel, qc, pair * 2 + 1)
        comm_step(33 + it)
        return carry

    lax.fori_loop(0, 8, attend_body, 0)
    sent = w.at[0, 0, pl.ds(0, NSTEP * PIECE)]
    pltpu.make_async_copy(sent, sent, ici_send.at[0]).wait()
    pltpu.make_async_copy(w.at[0, 0], w.at[0, 0], part_send.at[0]).wait()

    def tile_of(n):
        u, mine = n // 2, n % 2 == 0
        by_x = jnp.where(mine, c, 1 - c) == 0
        other = jnp.where(by_x, pick(u, (1, 0, 1, 1, 0, 0, 1, 0)), pick(u, (1, 1, 1, 0, 0, 1, 0, 0)))
        dz = jnp.where(by_x, pick(u, (0, 0, 3, 1, 3, 1, 2, 2)), pick(u, (0, 3, 1, 0, 3, 2, 1, 2)))
        core = jnp.where(mine, c, 1 - c)
        return ((z + dz) % 4) * 4 + ((xl + other) % 2) * 2 + core

    def tile_rows(n):
        return pl.ds(pl.multiple_of(tile_of(n) * PIECE, 16), PIECE)

    def relay_copy(n, device):
        rows = tile_rows(n)
        return pltpu.make_async_remote_copy(
            src_ref=w.at[0, 0, rows, pl.ds(0, 128)], dst_ref=relay.at[rows],
            send_sem=rs_send, recv_sem=relay_recv.at[n], device_id=device, device_id_type=MESH,
        )

    def sum_copy(n, rel, side, device):
        rows = tile_rows(n)
        return pltpu.make_async_remote_copy(
            src_ref=w.at[0, 0, rows, pl.ds(rel * 128, 128)], dst_ref=rbuf.at[side, rows],
            send_sem=rs_send, recv_sem=rs_recv.at[side, n], device_id=device, device_id_type=MESH,
        )

    def out_body(n, carry):
        @pl.when((n % 2 == 0) & (n >= 8) & (n < NT))
        def _():
            comm_step(37 + n // 2)

        @pl.when((n % 2 == 1) & (n < NT))
        def _():
            u = n // 2
            by_x = c == 1
            one = jnp.where(by_x, pick(u, (0, 15, 5, 6, 2, 3, 10, 9)), pick(u, (2, 5, 7, 15, 0, 11, 1, 4)))
            two = jnp.where(by_x, pick(u, (1, 4, 7, 8, 11, 12, 13, 14)), pick(u, (3, 6, 8, 9, 10, 12, 13, 14)))
            await_partner(2, one, 1)
            await_partner(2, two, 1)

        @pl.when(n < NT)
        def _():
            rows = tile_rows(n)
            dims = (((1,), (1,)), ((), ()))
            part = lax.dot_general(w[2, 0, rows, :], att[0], dims, preferred_element_type=F32)
            part += lax.dot_general(w[2, 1, rows, :], att[1], dims, preferred_element_type=F32)
            w[0, 0, rows, :] = part.astype(BF)

            @pl.when(n % 2 == 0)
            def _():
                relay_copy(n, yp).start()
                sum_copy(n, 2, 1, ym).start()

            @pl.when(n % 2 == 1)
            def _():
                relay_copy(n, ym).start()
                sum_copy(n, 1, 0, yp).start()

        @pl.when(n >= LAG)
        def _():
            m = n - LAG
            rows = tile_rows(m)
            relay_copy(m, yp).wait_recv()

            @pl.when(m % 2 == 0)
            def _():
                merged = w[0, 0, rows, pl.ds(128, 128)].astype(F32) + relay[rows].astype(F32)
                w[0, 0, rows, pl.ds(128, 128)] = merged.astype(BF)
                sum_copy(m, 1, 0, yp).start()

            @pl.when(m % 2 == 1)
            def _():
                merged = w[0, 0, rows, pl.ds(256, 128)].astype(F32) + relay[rows].astype(F32)
                w[0, 0, rows, pl.ds(256, 128)] = merged.astype(BF)
                sum_copy(m, 2, 1, ym).start()

        return carry

    lax.fori_loop(0, NT + LAG, out_body, 0)

    def sum_body(n, total):
        rows = tile_rows(n)
        sum_copy(n, 1, 0, yp).wait_recv()
        sum_copy(n, 2, 1, ym).wait_recv()
        value = (
            w[0, 0, rows, pl.ds(384, 128)].astype(F32)
            + rbuf[0, rows].astype(F32)
            + rbuf[1, rows].astype(F32)
        )
        padded = jnp.concatenate([value, jnp.zeros((48, 128), F32)], axis=0)
        proj[tile_of(n)] = padded.T
        return total + jnp.sum(value * value, axis=0, keepdims=True)

    total = lax.fori_loop(0, NT, sum_body, jnp.zeros((1, 128), F32))
    scale = lax.rsqrt(total * (1.0 / D) + EPS)
    scale = jnp.broadcast_to(scale, (128, 128)).T[:, 0:1]
    for t in range(NT):
        cols = slice(t * PIECE, (t + 1) * PIECE)
        out_ref[:, cols] = (
            hid_ref[:, cols].astype(F32) + proj[t][:, :PIECE] * scale * pg_ref[:, cols]
        ).astype(BF)

    for s in (1, 2):
        sent = w.at[s, 0, pl.ds(0, NSTEP * PIECE)]
        pltpu.make_async_copy(sent, sent, ici_send.at[s]).wait()
        pltpu.make_async_copy(w.at[s, 0], w.at[s, 0], part_send.at[s]).wait()
    halo = kv.at[:, :, pl.ds(0, 2 * TOK)]
    pltpu.make_async_copy(halo, halo, halo_send).wait()
    summed = act.at[pl.ds(0, 3)]
    pltpu.make_async_copy(summed, summed, rs_send).wait()
    pltpu.make_async_copy(summed, summed, act_send).wait()


def per_device(
    hidden_in, in_gain, query_weight, key_weight, value_weight, out_weight, q_gain, k_gain, post_gain
):
    ctx, tp = lax.axis_index("ctx"), lax.axis_index("tp")
    block = ctx * 2 + tp // 4
    positions = block * TOK + jnp.arange(TOK, dtype=jnp.int32)
    frequency = 10000.0 ** (-(jnp.arange(HEAD // 2, dtype=F32) * 2.0 / HEAD))
    angles = positions.astype(F32)[:, None] * frequency[None, :]
    cosine, sine = jnp.cos(angles), jnp.sin(angles)
    cos_table = jnp.concatenate([cosine, cosine], axis=-1)
    sin_table = jnp.concatenate([-sine, sine], axis=-1)
    vmem, hbm = pl.BlockSpec(memory_space=pltpu.VMEM), pl.BlockSpec(memory_space=pl.ANY)
    dma = pltpu.SemaphoreType.DMA
    return pl.pallas_call(
        kernel,
        out_shape=jax.ShapeDtypeStruct((128, D), BF),
        in_specs=[vmem, vmem, hbm, hbm, hbm, hbm, vmem, vmem, vmem, vmem, vmem],
        out_specs=vmem,
        scratch_shapes=[
            pltpu.VMEM((3, 2, D, 512), BF),
            pltpu.VMEM((4, 128, D), BF),
            pltpu.VMEM((2, 4, 3 * TOK, HEAD), BF),
            pltpu.VMEM((4, 2, TOK, HEAD), BF),
            pltpu.VMEM((2, TOK, 512), BF),
            pltpu.VMEM((2, TOK, 512), F32),
            pltpu.VMEM((4, 128, 1152), F32),
            pltpu.VMEM((D, 128), BF),
            pltpu.VMEM((2, D, 128), BF),
            pltpu.VMEM((NT, 128, 384), F32),
            dma((4,)), dma((3, NSTEP)), dma((3, NSTEP + 1)), dma((3,)), dma((3,)),
            dma((6,)), dma, dma((2, 2)), dma, dma((NT,)), dma((2, NT)), dma,
        ],
        compiler_params=pltpu.CompilerParams(
            collective_id=0, has_side_effects=True, vmem_limit_bytes=67043328
        ),
    )(
        hidden_in,
        in_gain.reshape(1, D),
        query_weight,
        key_weight,
        value_weight,
        out_weight.T,
        cos_table,
        sin_table,
        q_gain.reshape(1, HEAD),
        k_gain.reshape(1, HEAD),
        post_gain.reshape(1, D),
    )


def solution(mesh):
    in_specs = (
        P(("ctx", "tp"), None), P(), P("ctx", "tp"), P("ctx", "tp"), P("ctx", "tp"), P("tp", "ctx"),
        P(), P(), P(),
    )
    return jax.shard_map(
        per_device, mesh=mesh, in_specs=in_specs, out_specs=P(("ctx", "tp"), None), check_vma=False
    )
```

```python
import functools

import jax
import jax.numpy as jnp
from jax import lax
from jax.experimental import pallas as pl
from jax.experimental.pallas import tpu as pltpu
from jax.sharding import PartitionSpec as P

WINDOW = 1024
SCALE = 168.0 ** (-0.5)
EPS = 1e-06
D = 5376
PIECE = 336
TOK = 512
HEAD = 128
KCH = 768
NK = D // KCH
NT = 16
SUM_AT = 20
MESH = pl.DeviceIdType.MESH
BF = jnp.bfloat16
F32 = jnp.float32

STEP_A = (-1, 1, 0, 0, 2, -1, -1, 1, 1, 0, -1, 2, 2, 1, 2)
STEP_B = (0, 0, -1, 1, 0, -1, 1, -1, 1, 2, 2, -1, 1, 2, 2)
NSTEP = 15
OUT_START = 12
KV_STEPS = (0, 0, 0, 19, 0, 0, 0, 20, 0, 0, 0, 21, 0, 0)
KV_END = 22
HALO_AT = 27
Q_STEPS = (0, 0, 0, 0, 0, 0, 0, 30, 0, 31, 0, 32, 0, 33)
ATT_START = 34
GROUP = 8
Q_ORDER = (0, 2, 6, 1, 4, 3, 5, 2, 0, 4, 1, 3, 6, 5, 4, 2, 6, 3, 5, 0, 1, 6, 4, 0, 5, 2, 1, 3)
Q_OTHER = (0, 6, 1, 2, 3, 4, 5, 2, 0, 1, 3, 4, 5, 6, 4, 2, 3, 0, 1, 5, 6, 6, 4, 5, 0, 1, 2, 3)
LOG2E = 1.4426950408889634


def pick(k, values):
    out = jnp.int32(values[-1])
    for i in range(len(values) - 2, -1, -1):
        if values[i] != values[-1]:
            out = jnp.where(k == i, jnp.int32(values[i]), out)
    return out


def among(k, values):
    hit = k == values[0]
    for v in values[1:]:
        hit = hit | (k == v)
    return hit


def kernel(
    hid_ref, ing_ref, wq_ref, wk_ref, wv_ref, wo_ref, cos_ref, sin_ref, qg_ref, kg_ref, pg_ref,
    out_ref,
    w, act, kv, q, att, acc, bias, relay, rbuf, proj, squares,
    own_sem, ici_recv, part_recv, ici_send, pass_send, part_send,
    act_recv, act_send, halo_recv, halo_send, relay_recv, rs_recv, rs_send,
):
    ctx = lax.axis_index("ctx")
    tp = lax.axis_index("tp")
    z, xl, c = ctx // 4, (ctx // 2) % 2, ctx % 2
    xh, y = tp // 4, tp % 4
    x = xh * 2 + xl
    block = (z * 2 + xl) * 4 + c * 2 + xh

    def dev(dx, dz, core, dy):
        xx, zz, yy = (x + dx + 4) % 4, (z + dz + 4) % 4, (y + dy + 4) % 4
        return (zz * 4 + (xx % 2) * 2 + core, (xx // 2) * 4 + yy)

    def block_dev(b):
        return ((b // 8) * 4 + ((b // 4) % 2) * 2 + (b // 2) % 2, (b % 2) * 4 + y)

    yp, ym = dev(0, 0, c, 1), dev(0, 0, c, -1)
    partner = dev(0, 0, 1 - c, 0)
    ahead = [block_dev((block + 1) % 32), block_dev((block + 2) % 32)]
    behind = [block_dev((block + 31) % 32), block_dev((block + 30) % 32)]

    barrier = pltpu.get_barrier_semaphore()
    peers = [dev(1, 0, c, 0), dev(-1, 0, c, 0), dev(0, 1, c, 0), dev(0, -1, c, 0), yp, ym, partner]
    peers += ahead + behind
    for peer in peers:
        pl.semaphore_signal(barrier, inc=1, device_id=peer, device_id_type=MESH)

    own_rows = pl.ds(pl.multiple_of(ctx * PIECE, 16), PIECE)
    loads = [
        pltpu.make_async_copy(wk_ref, w.at[0, xh, own_rows, pl.ds(0, 256)], own_sem.at[0]),
        pltpu.make_async_copy(wv_ref, w.at[0, xh, own_rows, pl.ds(256, 256)], own_sem.at[1]),
        pltpu.make_async_copy(wq_ref, w.at[1, xh, own_rows], own_sem.at[2]),
        pltpu.make_async_copy(wo_ref, w.at[2, xh, own_rows], own_sem.at[3]),
    ]
    for load in loads:
        load.start()

    def x_first(s):
        return c == 0

    def axis_dev(s, first, sign):
        along_x = x_first(s) == first
        dx = jnp.where(along_x, sign, 0)
        dz = jnp.where(along_x, 0, sign)
        return dev(dx, dz, c, 0)

    def piece(s, da, db):
        fx = x_first(s)
        dx, dz = jnp.where(fx, da, db), jnp.where(fx, db, da)
        xx, zz = (x + dx + 4) % 4, (z + dz + 4) % 4
        row = pl.multiple_of((zz * 4 + (xx % 2) * 2 + c) * PIECE, 16)
        return w.at[s, xx // 2, pl.ds(row, PIECE)]

    def send(s, ref, device, at, sem):
        pltpu.make_async_remote_copy(
            src_ref=ref, dst_ref=ref, send_sem=sem, recv_sem=ici_recv.at[s, at],
            device_id=device, device_id_type=MESH,
        ).start()

    def send_partner(s, ref, k):
        late = jnp.where((s == 1) & (k > 12) & (k < NSTEP), 1, 0)
        pltpu.make_async_remote_copy(
            src_ref=ref, dst_ref=ref, send_sem=part_send.at[s],
            recv_sem=part_recv.at[s, jnp.where(s == 2, k, late)],
            device_id=partner, device_id_type=MESH,
        ).start()

    def start_own(s):
        ref = piece(s, 0, 0)
        send(s, ref, axis_dev(s, True, 1), 0, ici_send.at[s])
        send(s, ref, axis_dev(s, True, -1), 1, ici_send.at[s])
        send(s, ref, axis_dev(s, False, 1), 2, ici_send.at[s])
        send(s, ref, axis_dev(s, False, -1), 3, ici_send.at[s])
        send_partner(s, ref, NSTEP)

    def goes_plus(s, k):
        return jnp.where(k < 2, s % 2 == 0, among(k, (2, 3, 7, 8)))

    def passes_on(s, k):
        plus = goes_plus(s, k)
        up = among(k, (0, 2, 5, 7, 11)) & plus
        down = among(k, (1, 3, 6, 8, 12)) & jnp.logical_not(plus)
        return up, down

    def comm_step(g):
        s, k = g // NSTEP, g % NSTEP
        ref = piece(s, pick(k, STEP_A), pick(k, STEP_B))
        pltpu.make_async_copy(ref, ref, ici_recv.at[s, k]).wait()

        @pl.when(among(k, (0, 1, 4)))
        def _():
            at = pick(k, (5, 7, 0, 0, 11))
            send(s, ref, axis_dev(s, False, 1), at, ici_send.at[s])
            send(s, ref, axis_dev(s, False, -1), at + 1, ici_send.at[s])

        up, down = passes_on(s, k)

        @pl.when(up | down)
        def _():
            at = pick(k, (4, 4, 9, 9, 0, 10, 10, 13, 13, 0, 0, 14, 14))
            send(s, ref, axis_dev(s, k < 2, jnp.where(up, 1, -1)), at, pass_send.at[s, k])

        send_partner(s, ref, k)

        @pl.when(((k == 8) & (s == 0)) | ((k == OUT_START) & (s == 1)))
        def _():
            start_own(s + 1)

    def await_partner(s, at, count):
        ref = w.at[s, 0, pl.ds(0, count * PIECE)]
        pltpu.make_async_copy(ref, ref, part_recv.at[s, at]).wait()

    pl.semaphore_wait(barrier, len(peers))
    loads[0].wait()
    loads[1].wait()
    start_own(0)

    hid = hid_ref[...].astype(F32)
    mean = jnp.mean(hid * hid, axis=-1, keepdims=True)
    act[y] = (hid * lax.rsqrt(mean + EPS) * ing_ref[...]).astype(BF)
    loads[2].wait()
    loads[3].wait()

    def act_copy(owner, half, device, at):
        ref = act.at[owner, pl.ds(half * 64, 64)]
        return pltpu.make_async_remote_copy(
            src_ref=ref, dst_ref=ref, send_sem=act_send, recv_sem=act_recv.at[at],
            device_id=device, device_id_type=MESH,
        )

    act_copy(y, 0, yp, 0).start()
    act_copy(y, 1, ym, 3).start()
    act_copy(y, 1, yp, 1).start()
    act_copy(y, 0, ym, 2).start()
    before, after, across = (y + 3) % 4, (y + 1) % 4, (y + 2) % 4

    row = lax.broadcasted_iota(jnp.int32, (HEAD, 1152), 0)
    col = lax.broadcasted_iota(jnp.int32, (HEAD, 1152), 1)

    def mask_body(qc, carry):
        least = WINDOW - block * TOK - qc * 128
        allowed = (col > row) & (col <= row + WINDOW) & (col >= least)
        bias[qc] = jnp.where(allowed, 0.0, -1e30)
        return carry

    lax.fori_loop(0, 4, mask_body, 0)

    def stream_body(g, carry):
        comm_step(g)

        @pl.when(g == 8)
        def _():
            act_copy(before, 0, yp, 0).wait_recv()
            act_copy(before, 0, yp, 4).start()
            act_copy(after, 1, ym, 3).wait_recv()
            act_copy(after, 1, ym, 5).start()

        return carry

    lax.fori_loop(0, 19, stream_body, 0)
    act_copy(before, 1, yp, 1).wait_recv()
    act_copy(after, 0, ym, 2).wait_recv()
    act_copy(across, 0, yp, 4).wait_recv()
    act_copy(across, 1, ym, 5).wait_recv()
    await_partner(0, 0, 16)

    def project(s, half, kk, first):
        rows = pl.ds(pl.multiple_of(kk * KCH, KCH), KCH)
        left = act[:, :, rows].reshape(TOK, KCH)
        part = jnp.dot(left, w[s, half, rows, :], preferred_element_type=F32)

        @pl.when(first)
        def _():
            acc[half] = part

        @pl.when(jnp.logical_not(first))
        def _():
            acc[half] += part

    def normed_rope(vec, gain):
        mean = jnp.mean(vec * vec, axis=-1, keepdims=True)
        vec = vec * lax.rsqrt(mean + EPS) * gain
        return (vec * cos_ref[...] + pltpu.roll(vec, HEAD // 2, 1) * sin_ref[...]).astype(BF)

    def halo_copy(half, ahead_by):
        heads = pl.ds(half * 2, 2)
        return pltpu.make_async_remote_copy(
            src_ref=kv.at[:, heads, pl.ds(2 * TOK, TOK)],
            dst_ref=kv.at[:, heads, pl.ds((2 - ahead_by) * TOK, TOK)],
            send_sem=halo_send, recv_sem=halo_recv.at[ahead_by - 1, half],
            device_id=ahead[ahead_by - 1], device_id_type=MESH,
        )

    def kv_body(j, carry):
        half, kk = j // NK, j % NK
        project(0, half, kk, kk == 0)

        @pl.when(kk == NK - 1)
        def _():
            for h in range(2):
                kv[0, half * 2 + h, pl.ds(2 * TOK, TOK)] = normed_rope(
                    acc[half, :, h * HEAD : (h + 1) * HEAD], kg_ref[...]
                )
                kv[1, half * 2 + h, pl.ds(2 * TOK, TOK)] = acc[
                    half, :, (2 + h) * HEAD : (3 + h) * HEAD
                ].astype(BF)

        step = pick(j, KV_STEPS)

        @pl.when(step > 0)
        def _():
            comm_step(step)

        return carry

    def step_body(g, carry):
        comm_step(g)

        @pl.when(g == HALO_AT)
        def _():
            for half in range(2):
                halo_copy(half, 1).start()
                halo_copy(half, 2).start()

        return carry

    lax.fori_loop(0, 2 * NK, kv_body, 0)
    lax.fori_loop(KV_END, 28, step_body, 0)
    await_partner(1, 0, 14)

    def q_body(j, carry):
        mine = (j < 4) | ((j >= 6) & (j < 9))
        half = jnp.where(mine, xh, 1 - xh)
        p = pick(j, (0, 1, 2, 3, 0, 1, 4, 5, 6, 2, 3, 4, 5, 6))
        order = jnp.where(mine, pick(z * NK + p, Q_ORDER), pick(z * NK + p, Q_OTHER))

        @pl.when(j == 6)
        def _():
            lax.fori_loop(28, 30, step_body, 0)
            await_partner(1, 1, 2)

        project(1, half, order, p == 0)

        @pl.when(p == NK - 1)
        def _():
            for h in range(4):
                q[half * 2 + h // 2, h % 2] = normed_rope(
                    acc[half, :, h * HEAD : (h + 1) * HEAD], qg_ref[...]
                )

        step = pick(j, Q_STEPS)

        @pl.when(step > 0)
        def _():
            comm_step(step)

        return carry

    lax.fori_loop(0, 2 * NK, q_body, 0)
    lax.fori_loop(34, ATT_START, step_body, 0)
    for half in range(2):
        halo_copy(half, 1).wait_recv()
        halo_copy(half, 2).wait_recv()

    def attend(rel, qc, kvh):
        start = pl.multiple_of(qc * 128, 128)
        queries = q[kvh, :, pl.ds(start, 128), :].reshape(256, HEAD)
        keys = kv[0, kvh, pl.ds(start, 1152), :]
        values = kv[1, kvh, pl.ds(start, 1152), :]
        scores = lax.dot_general(
            queries, keys, (((1,), (1,)), ((), ())), preferred_element_type=F32
        )
        scores = scores.reshape(2, 128, 1152) * (SCALE * LOG2E) + bias[qc][None]
        expo = jnp.exp2(scores - jnp.max(scores, axis=-1, keepdims=True))
        weights = (expo * (1.0 / jnp.sum(expo, axis=-1, keepdims=True))).astype(BF)
        mixed = jnp.dot(weights.reshape(256, 1152), values, preferred_element_type=F32).astype(BF)
        rows = pl.ds(pl.multiple_of(rel * 128, 128), 128)
        for h in range(2):
            lanes = pl.ds(pl.multiple_of((kvh % 2) * 256 + h * 128, 128), 128)
            att[kvh // 2, rows, lanes] = mixed[h * 128 : (h + 1) * 128]

    def attend_step(it):
        rel, pair = it // 2, it % 2
        qc = (y + pick(rel, (2, 0, 1, 3))) % 4
        attend(rel, qc, pair * 2)
        attend(rel, qc, pair * 2 + 1)

    def attend_body(it, carry):
        attend_step(it)
        comm_step(ATT_START + it)
        return carry

    lax.fori_loop(0, 4, attend_body, 0)
    def drain(s):
        sent = w.at[s, 0, pl.ds(0, 10 * PIECE)]
        pltpu.make_async_copy(sent, sent, ici_send.at[s]).wait()
        pltpu.make_async_copy(w.at[s, 0], w.at[s, 0], part_send.at[s]).wait()

        def drain_body(k, carry):
            up, down = passes_on(s, k)

            @pl.when(up | down)
            def _():
                one = w.at[s, 0, pl.ds(0, PIECE)]
                pltpu.make_async_copy(one, one, pass_send.at[s, k]).wait()

            return carry

        lax.fori_loop(0, NSTEP, drain_body, 0)

    drain(0)

    def tile_of(n):
        u, mine = n // 2, n % 2 == 0
        by_x = jnp.where(mine, c, 1 - c) == 0
        other = jnp.where(by_x, pick(u, (1, 0, 1, 1, 0, 0, 1, 0)), pick(u, (1, 1, 1, 0, 0, 1, 0, 0)))
        dz = jnp.where(by_x, pick(u, (0, 0, 3, 1, 3, 1, 2, 2)), pick(u, (0, 3, 1, 0, 3, 2, 1, 2)))
        core = jnp.where(mine, c, 1 - c)
        return ((z + dz) % 4) * 4 + ((xl + other) % 2) * 2 + core

    def tile_rows(n):
        return pl.ds(pl.multiple_of(tile_of(n) * PIECE, 16), PIECE)

    def relay_copy(n, device):
        rows = tile_rows(n)
        return pltpu.make_async_remote_copy(
            src_ref=w.at[0, 0, rows, pl.ds(0, 128)], dst_ref=relay.at[rows],
            send_sem=rs_send, recv_sem=relay_recv.at[n], device_id=device, device_id_type=MESH,
        )

    def sum_copy(n, lane, side, device):
        rows = tile_rows(n)
        return pltpu.make_async_remote_copy(
            src_ref=w.at[0, 1, rows, pl.ds(lane, 128)], dst_ref=rbuf.at[side, rows],
            send_sem=rs_send, recv_sem=rs_recv.at[side, n], device_id=device, device_id_type=MESH,
        )

    def product(n, base):
        rows = tile_rows(n)
        dims = (((1,), (1,)), ((), ()))
        tokens = slice(base, base + 256)
        part = lax.dot_general(w[2, 0, rows, :], att[0, tokens], dims, preferred_element_type=F32)
        return part + lax.dot_general(
            w[2, 1, rows, :], att[1, tokens], dims, preferred_element_type=F32
        )

    def first_pass(n):
        u = n // 2

        @pl.when(n % 2 == 0)
        def _():
            lax.fori_loop(
                jnp.maximum(pick(u, (30, 34, 37, 39, 40, 42, 43, 44)), ATT_START + 4),
                jnp.maximum(pick(u, (34, 37, 39, 40, 42, 43, 44, 45)), ATT_START + 4),
                step_body, 0,
            )

        @pl.when(n % 2 == 1)
        def _():
            by_x = c == 1
            one = jnp.where(by_x, pick(u, (0, 15, 5, 6, 2, 3, 10, 9)), pick(u, (2, 5, 7, 15, 0, 11, 1, 4)))
            two = jnp.where(by_x, pick(u, (1, 4, 7, 8, 11, 12, 13, 14)), pick(u, (3, 6, 8, 9, 10, 12, 13, 14)))
            await_partner(2, one, 1)
            await_partner(2, two, 1)

        w[0, 0, tile_rows(n), pl.ds(0, 256)] = product(n, 0).astype(BF)

        @pl.when(n % 2 == 0)
        def _():
            relay_copy(n, yp).start()

        @pl.when(n % 2 == 1)
        def _():
            relay_copy(n, ym).start()

        @pl.when((n < 8) & (n % 2 == 1))
        def _():
            attend_step(4 + n // 2)

    def second_pass(n):
        rows = tile_rows(n)
        relay_copy(n, yp).wait_recv()
        part = product(n, 256)
        term = relay[rows].astype(F32)
        even = n % 2 == 0
        w[0, 1, rows, pl.ds(0, 128)] = (part[:, :128] + jnp.where(even, term, 0.0)).astype(BF)
        w[0, 1, rows, pl.ds(128, 128)] = (part[:, 128:] + jnp.where(even, 0.0, term)).astype(BF)
        sum_copy(n, 0, 0, yp).start()
        sum_copy(n, 128, 1, ym).start()

    def take_sum(m):
        rows = tile_rows(m)
        sum_copy(m, 0, 0, yp).wait_recv()
        sum_copy(m, 128, 1, ym).wait_recv()
        value = (
            w[0, 0, rows, pl.ds(128, 128)].astype(F32)
            + rbuf[0, rows].astype(F32)
            + rbuf[1, rows].astype(F32)
        )
        padded = jnp.concatenate([value, jnp.zeros((48, 128), F32)], axis=0)
        proj[tile_of(m)] = padded.T
        squares[...] += jnp.sum(value * value, axis=0, keepdims=True)

    def out_body(i, carry):
        group, at = i // (2 * GROUP), i % (2 * GROUP)
        n = group * GROUP + at % GROUP

        @pl.when((i < 2 * NT) & (at < GROUP))
        def _():
            first_pass(n)

        @pl.when((i < 2 * NT) & (at >= GROUP))
        def _():
            second_pass(n)

        @pl.when(i >= SUM_AT)
        def _():
            take_sum(i - SUM_AT)

        return carry

    squares[...] = jnp.zeros((1, 128), F32)
    lax.fori_loop(0, SUM_AT + NT, out_body, 0)
    scale = lax.rsqrt(squares[...] * (1.0 / D) + EPS)
    scale = jnp.broadcast_to(scale, (128, 128)).T[:, 0:1]
    for t in range(NT):
        cols = slice(t * PIECE, (t + 1) * PIECE)
        out_ref[:, cols] = (
            hid_ref[:, cols].astype(F32) + proj[t][:, :PIECE] * scale * pg_ref[:, cols]
        ).astype(BF)

    drain(1)
    drain(2)
    halo = kv.at[:, :, pl.ds(0, 2 * TOK)]
    pltpu.make_async_copy(halo, halo, halo_send).wait()
    summed = act.at[pl.ds(0, 3)]
    pltpu.make_async_copy(summed, summed, rs_send).wait()
    pltpu.make_async_copy(summed, summed, act_send).wait()


def per_device(
    hidden_in, in_gain, query_weight, key_weight, value_weight, out_weight, q_gain, k_gain, post_gain
):
    ctx, tp = lax.axis_index("ctx"), lax.axis_index("tp")
    block = ctx * 2 + tp // 4
    positions = block * TOK + jnp.arange(TOK, dtype=jnp.int32)
    frequency = 10000.0 ** (-(jnp.arange(HEAD // 2, dtype=F32) * 2.0 / HEAD))
    angles = positions.astype(F32)[:, None] * frequency[None, :]
    cosine, sine = jnp.cos(angles), jnp.sin(angles)
    cos_table = jnp.concatenate([cosine, cosine], axis=-1)
    sin_table = jnp.concatenate([-sine, sine], axis=-1)
    vmem, hbm = pl.BlockSpec(memory_space=pltpu.VMEM), pl.BlockSpec(memory_space=pl.ANY)
    dma = pltpu.SemaphoreType.DMA
    return pl.pallas_call(
        kernel,
        out_shape=jax.ShapeDtypeStruct((128, D), BF),
        in_specs=[vmem, vmem, hbm, hbm, hbm, hbm, vmem, vmem, vmem, vmem, vmem],
        out_specs=vmem,
        scratch_shapes=[
            pltpu.VMEM((3, 2, D, 512), BF),
            pltpu.VMEM((4, 128, D), BF),
            pltpu.VMEM((2, 4, 3 * TOK, HEAD), BF),
            pltpu.VMEM((4, 2, TOK, HEAD), BF),
            pltpu.VMEM((2, TOK, 512), BF),
            pltpu.VMEM((2, TOK, 512), F32),
            pltpu.VMEM((4, 128, 1152), F32),
            pltpu.VMEM((D, 128), BF),
            pltpu.VMEM((2, D, 128), BF),
            pltpu.VMEM((NT, 128, 384), F32),
            pltpu.VMEM((1, 128), F32),
            dma((4,)), dma((3, NSTEP)), dma((3, NSTEP + 1)), dma((3,)), dma((3, NSTEP)), dma((3,)),
            dma((6,)), dma, dma((2, 2)), dma, dma((NT,)), dma((2, NT)), dma,
        ],
        compiler_params=pltpu.CompilerParams(
            collective_id=0, has_side_effects=True, vmem_limit_bytes=67043328
        ),
    )(
        hidden_in,
        in_gain.reshape(1, D),
        query_weight,
        key_weight,
        value_weight,
        out_weight.T,
        cos_table,
        sin_table,
        q_gain.reshape(1, HEAD),
        k_gain.reshape(1, HEAD),
        post_gain.reshape(1, D),
    )


def solution(mesh):
    in_specs = (
        P(("ctx", "tp"), None), P(), P("ctx", "tp"), P("ctx", "tp"), P("ctx", "tp"), P("tp", "ctx"),
        P(), P(), P(),
    )
    return jax.shard_map(
        per_device, mesh=mesh, in_specs=in_specs, out_specs=P(("ctx", "tp"), None), check_vma=False
    )
```

```python
import functools

import jax
import jax.numpy as jnp
from jax import lax
from jax.experimental import pallas as pl
from jax.experimental.pallas import tpu as pltpu
from jax.sharding import PartitionSpec as P

WINDOW = 1024
SCALE = 168.0 ** (-0.5)
EPS = 1e-06
D = 5376
PIECE = 336
TOK = 512
HEAD = 128
KCH = 768
NK = D // KCH
NT = 16
SUM_AT = 22
MESH = pl.DeviceIdType.MESH
BF = jnp.bfloat16
F32 = jnp.float32

STEP_A = (-1, 1, 0, 0, 2, -1, -1, 1, 1, 0, -1, 2, 2, 1, 2)
STEP_B = (0, 0, -1, 1, 0, -1, 1, -1, 1, 2, 2, -1, 1, 2, 2)
NSTEP = 15
OUT_START = 12
KV_STEPS = (0, 0, 0, 19, 0, 0, 0, 20, 0, 0, 0, 21, 0, 0)
KV_END = 22
HALO_AT = 27
Q_STEPS = (0, 0, 0, 0, 0, 0, 0, 30, 0, 31, 0, 32, 0, 33)
ATT_START = 34
ATT_EACH = 1
OUT_STEPS = (0, 0, 38, 0, 0, 39, 0, 0, 0, 40, 0, 0, 0, 41, 0, 0, 0, 42, 0, 0, 43, 0, 0, 0, 44, 0)
Q_ORDER = (0, 2, 6, 1, 4, 3, 5, 2, 0, 4, 1, 3, 6, 5, 4, 2, 6, 3, 5, 0, 1, 6, 4, 0, 5, 2, 1, 3)
Q_OTHER = (0, 6, 1, 2, 3, 4, 5, 2, 0, 1, 3, 4, 5, 6, 4, 2, 3, 0, 1, 5, 6, 6, 4, 5, 0, 1, 2, 3)
LOG2E = 1.4426950408889634


def pick(k, values):
    out = jnp.int32(values[-1])
    for i in range(len(values) - 2, -1, -1):
        if values[i] != values[-1]:
            out = jnp.where(k == i, jnp.int32(values[i]), out)
    return out


def among(k, values):
    hit = k == values[0]
    for v in values[1:]:
        hit = hit | (k == v)
    return hit


def kernel(
    hid_ref, ing_ref, wq_ref, wk_ref, wv_ref, wo_ref, cos_ref, sin_ref, qg_ref, kg_ref, pg_ref,
    out_ref,
    w, act, kv, q, att, acc, bias, relay, rbuf, proj, squares,
    own_sem, ici_recv, part_recv, ici_send, pass_send, part_send,
    act_recv, act_send, halo_recv, halo_send, relay_recv, rs_recv, rs_send,
):
    ctx = lax.axis_index("ctx")
    tp = lax.axis_index("tp")
    z, xl, c = ctx // 4, (ctx // 2) % 2, ctx % 2
    xh, y = tp // 4, tp % 4
    x = xh * 2 + xl
    block = (z * 2 + xl) * 4 + c * 2 + xh

    def dev(dx, dz, core, dy):
        xx, zz, yy = (x + dx + 4) % 4, (z + dz + 4) % 4, (y + dy + 4) % 4
        return (zz * 4 + (xx % 2) * 2 + core, (xx // 2) * 4 + yy)

    def block_dev(b):
        return ((b // 8) * 4 + ((b // 4) % 2) * 2 + (b // 2) % 2, (b % 2) * 4 + y)

    yp, ym = dev(0, 0, c, 1), dev(0, 0, c, -1)
    partner = dev(0, 0, 1 - c, 0)
    ahead = [block_dev((block + 1) % 32), block_dev((block + 2) % 32)]
    behind = [block_dev((block + 31) % 32), block_dev((block + 30) % 32)]

    barrier = pltpu.get_barrier_semaphore()
    peers = [dev(1, 0, c, 0), dev(-1, 0, c, 0), dev(0, 1, c, 0), dev(0, -1, c, 0), yp, ym, partner]
    peers += ahead + behind
    for peer in peers:
        pl.semaphore_signal(barrier, inc=1, device_id=peer, device_id_type=MESH)

    own_rows = pl.ds(pl.multiple_of(ctx * PIECE, 16), PIECE)
    loads = [
        pltpu.make_async_copy(wk_ref, w.at[0, xh, own_rows, pl.ds(0, 256)], own_sem.at[0]),
        pltpu.make_async_copy(wv_ref, w.at[0, xh, own_rows, pl.ds(256, 256)], own_sem.at[1]),
        pltpu.make_async_copy(wq_ref, w.at[1, xh, own_rows], own_sem.at[2]),
        pltpu.make_async_copy(wo_ref, w.at[2, xh, own_rows], own_sem.at[3]),
    ]
    for load in loads:
        load.start()

    def x_first(s):
        return c == 0

    def axis_dev(s, first, sign):
        along_x = x_first(s) == first
        dx = jnp.where(along_x, sign, 0)
        dz = jnp.where(along_x, 0, sign)
        return dev(dx, dz, c, 0)

    def piece(s, da, db):
        fx = x_first(s)
        dx, dz = jnp.where(fx, da, db), jnp.where(fx, db, da)
        xx, zz = (x + dx + 4) % 4, (z + dz + 4) % 4
        row = pl.multiple_of((zz * 4 + (xx % 2) * 2 + c) * PIECE, 16)
        return w.at[s, xx // 2, pl.ds(row, PIECE)]

    def send(s, ref, device, at, sem):
        pltpu.make_async_remote_copy(
            src_ref=ref, dst_ref=ref, send_sem=sem, recv_sem=ici_recv.at[s, at],
            device_id=device, device_id_type=MESH,
        ).start()

    def send_partner(s, ref, k):
        late = jnp.where((s == 1) & (k > 12) & (k < NSTEP), 1, 0)
        pltpu.make_async_remote_copy(
            src_ref=ref, dst_ref=ref, send_sem=part_send.at[s],
            recv_sem=part_recv.at[s, jnp.where(s == 2, k, late)],
            device_id=partner, device_id_type=MESH,
        ).start()

    def start_own(s):
        ref = piece(s, 0, 0)
        send(s, ref, axis_dev(s, True, 1), 0, ici_send.at[s])
        send(s, ref, axis_dev(s, True, -1), 1, ici_send.at[s])
        send(s, ref, axis_dev(s, False, 1), 2, ici_send.at[s])
        send(s, ref, axis_dev(s, False, -1), 3, ici_send.at[s])
        send_partner(s, ref, NSTEP)

    def goes_plus(s, k):
        return jnp.where(k < 2, s % 2 == 0, among(k, (2, 3, 7, 8)))

    def passes_on(s, k):
        plus = goes_plus(s, k)
        up = among(k, (0, 2, 5, 7, 11)) & plus
        down = among(k, (1, 3, 6, 8, 12)) & jnp.logical_not(plus)
        return up, down

    def comm_step(g):
        s, k = g // NSTEP, g % NSTEP
        ref = piece(s, pick(k, STEP_A), pick(k, STEP_B))
        pltpu.make_async_copy(ref, ref, ici_recv.at[s, k]).wait()

        @pl.when(among(k, (0, 1, 4)))
        def _():
            at = pick(k, (5, 7, 0, 0, 11))
            send(s, ref, axis_dev(s, False, 1), at, ici_send.at[s])
            send(s, ref, axis_dev(s, False, -1), at + 1, ici_send.at[s])

        up, down = passes_on(s, k)

        @pl.when(up | down)
        def _():
            at = pick(k, (4, 4, 9, 9, 0, 10, 10, 13, 13, 0, 0, 14, 14))
            send(s, ref, axis_dev(s, k < 2, jnp.where(up, 1, -1)), at, pass_send.at[s, k])

        send_partner(s, ref, k)

        @pl.when(((k == 8) & (s == 0)) | ((k == OUT_START) & (s == 1)))
        def _():
            start_own(s + 1)

    def await_partner(s, at, count):
        ref = w.at[s, 0, pl.ds(0, count * PIECE)]
        pltpu.make_async_copy(ref, ref, part_recv.at[s, at]).wait()

    pl.semaphore_wait(barrier, len(peers))
    loads[0].wait()
    loads[1].wait()
    start_own(0)

    hid = hid_ref[...].astype(F32)
    mean = jnp.mean(hid * hid, axis=-1, keepdims=True)
    act[y] = (hid * lax.rsqrt(mean + EPS) * ing_ref[...].reshape(1, D)).astype(BF)
    loads[2].wait()
    loads[3].wait()

    def act_copy(owner, half, device, at):
        ref = act.at[owner, pl.ds(half * 64, 64)]
        return pltpu.make_async_remote_copy(
            src_ref=ref, dst_ref=ref, send_sem=act_send, recv_sem=act_recv.at[at],
            device_id=device, device_id_type=MESH,
        )

    act_copy(y, 0, yp, 0).start()
    act_copy(y, 1, ym, 3).start()
    act_copy(y, 1, yp, 1).start()
    act_copy(y, 0, ym, 2).start()
    before, after, across = (y + 3) % 4, (y + 1) % 4, (y + 2) % 4

    row = lax.broadcasted_iota(jnp.int32, (HEAD, 1152), 0)
    col = lax.broadcasted_iota(jnp.int32, (HEAD, 1152), 1)

    def mask_body(qc, carry):
        least = WINDOW - block * TOK - qc * 128
        allowed = (col > row) & (col <= row + WINDOW) & (col >= least)
        bias[qc] = jnp.where(allowed, 0.0, -1e30)
        return carry

    lax.fori_loop(0, 4, mask_body, 0)

    def stream_body(g, carry):
        comm_step(g)

        @pl.when(g == 8)
        def _():
            act_copy(before, 0, yp, 0).wait_recv()
            act_copy(before, 0, yp, 4).start()
            act_copy(after, 1, ym, 3).wait_recv()
            act_copy(after, 1, ym, 5).start()

        return carry

    lax.fori_loop(0, 19, stream_body, 0)
    act_copy(before, 1, yp, 1).wait_recv()
    act_copy(after, 0, ym, 2).wait_recv()
    act_copy(across, 0, yp, 4).wait_recv()
    act_copy(across, 1, ym, 5).wait_recv()
    await_partner(0, 0, 16)

    def project(s, half, kk, first):
        rows = pl.ds(pl.multiple_of(kk * KCH, KCH), KCH)
        left = act[:, :, rows].reshape(TOK, KCH)
        part = jnp.dot(left, w[s, half, rows, :], preferred_element_type=F32)

        @pl.when(first)
        def _():
            acc[half] = part

        @pl.when(jnp.logical_not(first))
        def _():
            acc[half] += part

    def normed_rope(vec, gain):
        mean = jnp.mean(vec * vec, axis=-1, keepdims=True)
        vec = vec * lax.rsqrt(mean + EPS) * gain
        return (vec * cos_ref[...] + pltpu.roll(vec, HEAD // 2, 1) * sin_ref[...]).astype(BF)

    def halo_copy(half, ahead_by):
        heads = pl.ds(half * 2, 2)
        return pltpu.make_async_remote_copy(
            src_ref=kv.at[:, heads, pl.ds(2 * TOK, TOK)],
            dst_ref=kv.at[:, heads, pl.ds((2 - ahead_by) * TOK, TOK)],
            send_sem=halo_send, recv_sem=halo_recv.at[ahead_by - 1, half],
            device_id=ahead[ahead_by - 1], device_id_type=MESH,
        )

    def kv_body(j, carry):
        half, kk = j // NK, j % NK
        project(0, half, kk, kk == 0)

        @pl.when(kk == NK - 1)
        def _():
            for h in range(2):
                kv[0, half * 2 + h, pl.ds(2 * TOK, TOK)] = normed_rope(
                    acc[half, :, h * HEAD : (h + 1) * HEAD], kg_ref[...]
                )
                kv[1, half * 2 + h, pl.ds(2 * TOK, TOK)] = acc[
                    half, :, (2 + h) * HEAD : (3 + h) * HEAD
                ].astype(BF)

        step = pick(j, KV_STEPS)

        @pl.when(step > 0)
        def _():
            comm_step(step)

        return carry

    def step_body(g, carry):
        comm_step(g)

        @pl.when(g == HALO_AT)
        def _():
            for half in range(2):
                halo_copy(half, 1).start()
                halo_copy(half, 2).start()

        return carry

    lax.fori_loop(0, 2 * NK, kv_body, 0)
    lax.fori_loop(KV_END, 28, step_body, 0)
    await_partner(1, 0, 14)

    def q_body(j, carry):
        mine = (j < 4) | ((j >= 6) & (j < 9))
        half = jnp.where(mine, xh, 1 - xh)
        p = pick(j, (0, 1, 2, 3, 0, 1, 4, 5, 6, 2, 3, 4, 5, 6))
        order = jnp.where(mine, pick(z * NK + p, Q_ORDER), pick(z * NK + p, Q_OTHER))

        @pl.when(j == 6)
        def _():
            lax.fori_loop(28, 30, step_body, 0)
            await_partner(1, 1, 2)

        project(1, half, order, p == 0)

        @pl.when(p == NK - 1)
        def _():
            for h in range(4):
                q[half * 2 + h // 2, h % 2] = normed_rope(
                    acc[half, :, h * HEAD : (h + 1) * HEAD], qg_ref[...]
                )

        step = pick(j, Q_STEPS)

        @pl.when(step > 0)
        def _():
            comm_step(step)

        return carry

    lax.fori_loop(0, 2 * NK, q_body, 0)
    lax.fori_loop(34, ATT_START, step_body, 0)
    for half in range(2):
        halo_copy(half, 1).wait_recv()
        halo_copy(half, 2).wait_recv()

    def attend(rel, qc, kvh):
        start = pl.multiple_of(qc * 128, 128)
        queries = q[kvh, :, pl.ds(start, 128), :].reshape(256, HEAD)
        keys = kv[0, kvh, pl.ds(start, 1152), :]
        values = kv[1, kvh, pl.ds(start, 1152), :]
        scores = lax.dot_general(
            queries, keys, (((1,), (1,)), ((), ())), preferred_element_type=F32
        )
        scores = scores.reshape(2, 128, 1152) * (SCALE * LOG2E) + bias[qc][None]
        expo = jnp.exp2(scores - jnp.max(scores, axis=-1, keepdims=True))
        weights = (expo * (1.0 / jnp.sum(expo, axis=-1, keepdims=True))).astype(BF)
        mixed = jnp.dot(weights.reshape(256, 1152), values, preferred_element_type=F32).astype(BF)
        rows = pl.ds(pl.multiple_of(rel * 128, 128), 128)
        for h in range(2):
            lanes = pl.ds(pl.multiple_of((kvh % 2) * 256 + h * 128, 128), 128)
            att[kvh // 2, rows, lanes] = mixed[h * 128 : (h + 1) * 128]

    def attend_step(it):
        rel, pair = it // 2, it % 2
        qc = (y + pick(rel, (2, 0, 1, 3))) % 4
        attend(rel, qc, pair * 2)
        attend(rel, qc, pair * 2 + 1)

    def attend_body(it, carry):
        attend_step(it)
        lax.fori_loop(ATT_START + ATT_EACH * it, ATT_START + ATT_EACH * (it + 1), step_body, 0)
        return carry

    lax.fori_loop(0, 4, attend_body, 0)
    def drain(s):
        sent = w.at[s, 0, pl.ds(0, 10 * PIECE)]
        pltpu.make_async_copy(sent, sent, ici_send.at[s]).wait()
        pltpu.make_async_copy(w.at[s, 0], w.at[s, 0], part_send.at[s]).wait()

        def drain_body(k, carry):
            up, down = passes_on(s, k)

            @pl.when(up | down)
            def _():
                one = w.at[s, 0, pl.ds(0, PIECE)]
                pltpu.make_async_copy(one, one, pass_send.at[s, k]).wait()

            return carry

        lax.fori_loop(0, NSTEP, drain_body, 0)

    drain(0)

    def tile_of(n):
        u, mine = n // 2, n % 2 == 0
        by_x = jnp.where(mine, c, 1 - c) == 0
        other = jnp.where(by_x, pick(u, (1, 0, 1, 1, 0, 0, 1, 0)), pick(u, (1, 1, 1, 0, 0, 1, 0, 0)))
        dz = jnp.where(by_x, pick(u, (0, 0, 3, 1, 3, 1, 2, 2)), pick(u, (0, 3, 1, 0, 3, 2, 1, 2)))
        core = jnp.where(mine, c, 1 - c)
        return ((z + dz) % 4) * 4 + ((xl + other) % 2) * 2 + core

    def tile_rows(n):
        return pl.ds(pl.multiple_of(tile_of(n) * PIECE, 16), PIECE)

    def relay_copy(n, device):
        rows = tile_rows(n)
        return pltpu.make_async_remote_copy(
            src_ref=w.at[0, 0, rows, pl.ds(0, 128)], dst_ref=relay.at[rows],
            send_sem=rs_send, recv_sem=relay_recv.at[n], device_id=device, device_id_type=MESH,
        )

    def sum_copy(n, lane, side, device):
        rows = tile_rows(n)
        return pltpu.make_async_remote_copy(
            src_ref=w.at[0, 1, rows, pl.ds(lane, 128)], dst_ref=rbuf.at[side, rows],
            send_sem=rs_send, recv_sem=rs_recv.at[side, n], device_id=device, device_id_type=MESH,
        )

    def product(n, base):
        rows = tile_rows(n)
        dims = (((1,), (1,)), ((), ()))
        tokens = slice(base, base + 256)
        part = lax.dot_general(w[2, 0, rows, :], att[0, tokens], dims, preferred_element_type=F32)
        return part + lax.dot_general(
            w[2, 1, rows, :], att[1, tokens], dims, preferred_element_type=F32
        )

    def first_pass(n):
        u = n // 2

        @pl.when(n % 2 == 1)
        def _():
            by_x = c == 1
            one = jnp.where(by_x, pick(u, (0, 15, 5, 6, 2, 3, 10, 9)), pick(u, (2, 5, 7, 15, 0, 11, 1, 4)))
            two = jnp.where(by_x, pick(u, (1, 4, 7, 8, 11, 12, 13, 14)), pick(u, (3, 6, 8, 9, 10, 12, 13, 14)))
            await_partner(2, one, 1)
            await_partner(2, two, 1)

        w[0, 0, tile_rows(n), pl.ds(0, 256)] = product(n, 0).astype(BF)

        @pl.when(n % 2 == 0)
        def _():
            relay_copy(n, yp).start()

        @pl.when(n % 2 == 1)
        def _():
            relay_copy(n, ym).start()

        @pl.when((n < 8) & (n % 2 == 1))
        def _():
            attend_step(4 + n // 2)

    def second_pass(n):
        rows = tile_rows(n)
        relay_copy(n, yp).wait_recv()
        part = product(n, 256)
        term = relay[rows].astype(F32)
        even = n % 2 == 0
        w[0, 1, rows, pl.ds(0, 128)] = (part[:, :128] + jnp.where(even, term, 0.0)).astype(BF)
        w[0, 1, rows, pl.ds(128, 128)] = (part[:, 128:] + jnp.where(even, 0.0, term)).astype(BF)
        sum_copy(n, 0, 0, yp).start()
        sum_copy(n, 128, 1, ym).start()

    def take_sum(m):
        rows = tile_rows(m)
        sum_copy(m, 0, 0, yp).wait_recv()
        sum_copy(m, 128, 1, ym).wait_recv()
        value = (
            w[0, 0, rows, pl.ds(128, 128)].astype(F32)
            + rbuf[0, rows].astype(F32)
            + rbuf[1, rows].astype(F32)
        )
        padded = jnp.concatenate([value, jnp.zeros((48, 128), F32)], axis=0)
        proj[tile_of(m)] = padded.T
        squares[...] += jnp.sum(value * value, axis=0, keepdims=True)

    def out_body(i, carry):
        pair = (i - NT) // 2
        early = i < NT
        first = (early & (i < 8)) | among(pair, (0, 1, 3, 5))
        late = 2 * pick(pair, (4, 5, 4, 6, 5, 7, 6, 7)) + i % 2
        n = jnp.where(early, i % 8, late)
        step = pick(i, OUT_STEPS)

        @pl.when(step > 0)
        def _():
            comm_step(step)

        @pl.when((i < 2 * NT) & first)
        def _():
            first_pass(n)

        @pl.when((i < 2 * NT) & jnp.logical_not(first))
        def _():
            second_pass(n)

        @pl.when(i >= SUM_AT)
        def _():
            take_sum(i - SUM_AT)

        return carry

    squares[...] = jnp.zeros((1, 128), F32)
    lax.fori_loop(0, SUM_AT + NT, out_body, 0)
    scale = lax.rsqrt(squares[...] * (1.0 / D) + EPS)
    scale = jnp.broadcast_to(scale, (128, 128)).T[:, 0:1]
    post = pg_ref[...].reshape(1, D)
    for t in range(NT):
        cols = slice(t * PIECE, (t + 1) * PIECE)
        out_ref[:, cols] = (
            hid_ref[:, cols].astype(F32) + proj[t][:, :PIECE] * scale * post[:, cols]
        ).astype(BF)

    drain(1)
    drain(2)
    halo = kv.at[:, :, pl.ds(0, 2 * TOK)]
    pltpu.make_async_copy(halo, halo, halo_send).wait()
    summed = act.at[pl.ds(0, 3)]
    pltpu.make_async_copy(summed, summed, rs_send).wait()
    pltpu.make_async_copy(summed, summed, act_send).wait()


def per_device(
    hidden_in, in_gain, query_weight, key_weight, value_weight, out_weight, q_gain, k_gain, post_gain
):
    ctx, tp = lax.axis_index("ctx"), lax.axis_index("tp")
    block = ctx * 2 + tp // 4
    positions = block * TOK + jnp.arange(TOK, dtype=jnp.int32)
    frequency = 10000.0 ** (-(jnp.arange(HEAD // 2, dtype=F32) * 2.0 / HEAD))
    angles = positions.astype(F32)[:, None] * frequency[None, :]
    cosine, sine = jnp.cos(angles), jnp.sin(angles)
    cos_table = jnp.concatenate([cosine, cosine], axis=-1)
    sin_table = jnp.concatenate([-sine, sine], axis=-1)
    vmem, hbm = pl.BlockSpec(memory_space=pltpu.VMEM), pl.BlockSpec(memory_space=pl.ANY)
    dma = pltpu.SemaphoreType.DMA
    return pl.pallas_call(
        kernel,
        out_shape=jax.ShapeDtypeStruct((128, D), BF),
        in_specs=[vmem, vmem, hbm, hbm, hbm, hbm, vmem, vmem, vmem, vmem, vmem],
        out_specs=vmem,
        scratch_shapes=[
            pltpu.VMEM((3, 2, D, 512), BF),
            pltpu.VMEM((4, 128, D), BF),
            pltpu.VMEM((2, 4, 3 * TOK, HEAD), BF),
            pltpu.VMEM((4, 2, TOK, HEAD), BF),
            pltpu.VMEM((2, TOK, 512), BF),
            pltpu.VMEM((2, TOK, 512), F32),
            pltpu.VMEM((4, 128, 1152), F32),
            pltpu.VMEM((D, 128), BF),
            pltpu.VMEM((2, D, 128), BF),
            pltpu.VMEM((NT, 128, 384), F32),
            pltpu.VMEM((1, 128), F32),
            dma((4,)), dma((3, NSTEP)), dma((3, NSTEP + 1)), dma((3,)), dma((3, NSTEP)), dma((3,)),
            dma((6,)), dma, dma((2, 2)), dma, dma((NT,)), dma((2, NT)), dma,
        ],
        compiler_params=pltpu.CompilerParams(
            collective_id=0, has_side_effects=True, vmem_limit_bytes=67043328
        ),
    )(
        hidden_in,
        in_gain,
        query_weight,
        key_weight,
        value_weight,
        out_weight.T,
        cos_table,
        sin_table,
        q_gain.reshape(1, HEAD),
        k_gain.reshape(1, HEAD),
        post_gain,
    )


def solution(mesh):
    in_specs = (
        P(("ctx", "tp"), None), P(), P("ctx", "tp"), P("ctx", "tp"), P("ctx", "tp"), P("tp", "ctx"),
        P(), P(), P(),
    )
    return jax.shard_map(
        per_device, mesh=mesh, in_specs=in_specs, out_specs=P(("ctx", "tp"), None), check_vma=False
    )
```

```python
import functools

import jax
import jax.numpy as jnp
from jax import lax
from jax.experimental import pallas as pl
from jax.experimental.pallas import tpu as pltpu
from jax.sharding import PartitionSpec as P

WINDOW = 1024
SCALE = 168.0 ** (-0.5)
EPS = 1e-06
D = 5376
PIECE = 336
TOK = 512
HEAD = 128
KCH = 768
NK = D // KCH
NT = 16
SUM_AT = 22
MESH = pl.DeviceIdType.MESH
BF = jnp.bfloat16
F32 = jnp.float32

STEP_A = (-1, 1, 0, 0, 2, -1, -1, 1, 1, 0, -1, 2, 2, 1, 2)
STEP_B = (0, 0, -1, 1, 0, -1, 1, -1, 1, 2, 2, -1, 1, 2, 2)
NSTEP = 15
OUT_START = 12
KV_STEPS = (0, 0, 0, 19, 0, 0, 0, 20, 0, 0, 0, 21, 0, 0)
KV_END = 22
HALO_AT = 27
Q_STEPS = (0, 0, 0, 0, 0, 0, 0, 30, 0, 31, 0, 32, 0, 33)
ATT_START = 34
ATT_EACH = 1
OUT_STEPS = (0, 0, 38, 0, 0, 39, 0, 0, 0, 40, 0, 0, 0, 41, 0, 0, 0, 42, 0, 0, 43, 0, 0, 0, 44, 0)
Q_ORDER = (0, 2, 6, 1, 4, 3, 5, 2, 0, 4, 1, 3, 6, 5, 4, 2, 6, 3, 5, 0, 1, 6, 4, 0, 5, 2, 1, 3)
Q_OTHER = (0, 6, 1, 2, 3, 4, 5, 2, 0, 1, 3, 4, 5, 6, 4, 2, 3, 0, 1, 5, 6, 6, 4, 5, 0, 1, 2, 3)
LOG2E = 1.4426950408889634


def pick(k, values):
    out = jnp.int32(values[-1])
    for i in range(len(values) - 2, -1, -1):
        if values[i] != values[-1]:
            out = jnp.where(k == i, jnp.int32(values[i]), out)
    return out


def among(k, values):
    hit = k == values[0]
    for v in values[1:]:
        hit = hit | (k == v)
    return hit


def kernel(
    hid_ref, ing_ref, wq_ref, wk_ref, wv_ref, wo_ref, cos_ref, sin_ref, qg_ref, kg_ref, pg_ref,
    out_ref,
    w, act, kv, q, att, acc, bias, relay, rbuf, proj, squares,
    own_sem, ici_recv, part_recv, ici_send, pass_send, part_send,
    act_recv, act_send, halo_recv, halo_send, relay_recv, rs_recv, rs_send,
):
    ctx = lax.axis_index("ctx")
    tp = lax.axis_index("tp")
    z, xl, c = ctx // 4, (ctx // 2) % 2, ctx % 2
    xh, y = tp // 4, tp % 4
    x = xh * 2 + xl
    block = (z * 2 + xl) * 4 + c * 2 + xh

    def dev(dx, dz, core, dy):
        xx, zz, yy = (x + dx + 4) % 4, (z + dz + 4) % 4, (y + dy + 4) % 4
        return (zz * 4 + (xx % 2) * 2 + core, (xx // 2) * 4 + yy)

    def block_dev(b):
        return ((b // 8) * 4 + ((b // 4) % 2) * 2 + (b // 2) % 2, (b % 2) * 4 + y)

    yp, ym = dev(0, 0, c, 1), dev(0, 0, c, -1)
    partner = dev(0, 0, 1 - c, 0)
    ahead = [block_dev((block + 1) % 32), block_dev((block + 2) % 32)]
    behind = [block_dev((block + 31) % 32), block_dev((block + 30) % 32)]

    barrier = pltpu.get_barrier_semaphore()
    peers = [dev(1, 0, c, 0), dev(-1, 0, c, 0), dev(0, 1, c, 0), dev(0, -1, c, 0), yp, ym, partner]
    peers += ahead + behind
    for peer in peers:
        pl.semaphore_signal(barrier, inc=1, device_id=peer, device_id_type=MESH)

    own_rows = pl.ds(pl.multiple_of(ctx * PIECE, 16), PIECE)
    loads = [
        pltpu.make_async_copy(wk_ref, w.at[0, xh, own_rows, pl.ds(0, 256)], own_sem.at[0]),
        pltpu.make_async_copy(wv_ref, w.at[0, xh, own_rows, pl.ds(256, 256)], own_sem.at[1]),
        pltpu.make_async_copy(wq_ref, w.at[1, xh, own_rows], own_sem.at[2]),
        pltpu.make_async_copy(wo_ref, w.at[2, xh, own_rows], own_sem.at[3]),
    ]
    for load in loads:
        load.start()

    def x_first(s):
        return c == 0

    def axis_dev(s, first, sign):
        along_x = x_first(s) == first
        dx = jnp.where(along_x, sign, 0)
        dz = jnp.where(along_x, 0, sign)
        return dev(dx, dz, c, 0)

    def piece(s, da, db):
        fx = x_first(s)
        dx, dz = jnp.where(fx, da, db), jnp.where(fx, db, da)
        xx, zz = (x + dx + 4) % 4, (z + dz + 4) % 4
        row = pl.multiple_of((zz * 4 + (xx % 2) * 2 + c) * PIECE, 16)
        return w.at[s, xx // 2, pl.ds(row, PIECE)]

    def send(s, ref, device, at, sem):
        pltpu.make_async_remote_copy(
            src_ref=ref, dst_ref=ref, send_sem=sem, recv_sem=ici_recv.at[s, at],
            device_id=device, device_id_type=MESH,
        ).start()

    def send_partner(s, ref, k):
        late = jnp.where((s == 1) & (k > 12) & (k < NSTEP), 1, 0)
        pltpu.make_async_remote_copy(
            src_ref=ref, dst_ref=ref, send_sem=part_send.at[s],
            recv_sem=part_recv.at[s, jnp.where(s == 2, k, late)],
            device_id=partner, device_id_type=MESH,
        ).start()

    def start_own(s):
        ref = piece(s, 0, 0)
        send(s, ref, axis_dev(s, True, 1), 0, ici_send.at[s])
        send(s, ref, axis_dev(s, True, -1), 1, ici_send.at[s])
        send(s, ref, axis_dev(s, False, 1), 2, ici_send.at[s])
        send(s, ref, axis_dev(s, False, -1), 3, ici_send.at[s])
        send_partner(s, ref, NSTEP)

    def goes_plus(s, k):
        return jnp.where(k < 2, s % 2 == 0, among(k, (2, 3, 7, 8)))

    def passes_on(s, k):
        plus = goes_plus(s, k)
        up = among(k, (0, 2, 5, 7, 11)) & plus
        down = among(k, (1, 3, 6, 8, 12)) & jnp.logical_not(plus)
        return up, down

    def comm_step(g):
        s, k = g // NSTEP, g % NSTEP
        ref = piece(s, pick(k, STEP_A), pick(k, STEP_B))
        pltpu.make_async_copy(ref, ref, ici_recv.at[s, k]).wait()

        @pl.when(among(k, (0, 1, 4)))
        def _():
            at = pick(k, (5, 7, 0, 0, 11))
            send(s, ref, axis_dev(s, False, 1), at, ici_send.at[s])
            send(s, ref, axis_dev(s, False, -1), at + 1, ici_send.at[s])

        up, down = passes_on(s, k)

        @pl.when(up | down)
        def _():
            at = pick(k, (4, 4, 9, 9, 0, 10, 10, 13, 13, 0, 0, 14, 14))
            send(s, ref, axis_dev(s, k < 2, jnp.where(up, 1, -1)), at, pass_send.at[s, k])

        send_partner(s, ref, k)

        @pl.when(((k == 8) & (s == 0)) | ((k == OUT_START) & (s == 1)))
        def _():
            start_own(s + 1)

    def await_partner(s, at, count):
        ref = w.at[s, 0, pl.ds(0, count * PIECE)]
        pltpu.make_async_copy(ref, ref, part_recv.at[s, at]).wait()

    pl.semaphore_wait(barrier, len(peers))
    loads[0].wait()
    loads[1].wait()
    start_own(0)

    hid = hid_ref[...].astype(F32)
    mean = jnp.mean(hid * hid, axis=-1, keepdims=True)
    act[y] = (hid * lax.rsqrt(mean + EPS) * ing_ref[...].reshape(1, D)).astype(BF)
    loads[2].wait()
    loads[3].wait()

    def act_copy(owner, half, device, at):
        ref = act.at[owner, pl.ds(half * 64, 64)]
        return pltpu.make_async_remote_copy(
            src_ref=ref, dst_ref=ref, send_sem=act_send, recv_sem=act_recv.at[at],
            device_id=device, device_id_type=MESH,
        )

    act_copy(y, 0, yp, 0).start()
    act_copy(y, 1, ym, 3).start()
    act_copy(y, 1, yp, 1).start()
    act_copy(y, 0, ym, 2).start()
    before, after, across = (y + 3) % 4, (y + 1) % 4, (y + 2) % 4

    row = lax.broadcasted_iota(jnp.int32, (HEAD, 1152), 0)
    col = lax.broadcasted_iota(jnp.int32, (HEAD, 1152), 1)

    def mask_body(qc, carry):
        least = WINDOW - block * TOK - qc * 128
        allowed = (col > row) & (col <= row + WINDOW) & (col >= least)
        bias[qc] = jnp.where(allowed, 0.0, -1e30)
        return carry

    lax.fori_loop(0, 4, mask_body, 0)

    def stream_body(g, carry):
        comm_step(g)

        @pl.when(g == 8)
        def _():
            act_copy(before, 0, yp, 0).wait_recv()
            act_copy(before, 0, yp, 4).start()
            act_copy(after, 1, ym, 3).wait_recv()
            act_copy(after, 1, ym, 5).start()

        return carry

    lax.fori_loop(0, 19, stream_body, 0)
    act_copy(before, 1, yp, 1).wait_recv()
    act_copy(after, 0, ym, 2).wait_recv()
    act_copy(across, 0, yp, 4).wait_recv()
    act_copy(across, 1, ym, 5).wait_recv()
    await_partner(0, 0, 16)

    def project(s, half, kk, first):
        rows = pl.ds(pl.multiple_of(kk * KCH, KCH), KCH)
        left = act[:, :, rows].reshape(TOK, KCH)
        part = jnp.dot(left, w[s, half, rows, :], preferred_element_type=F32)

        @pl.when(first)
        def _():
            acc[half] = part

        @pl.when(jnp.logical_not(first))
        def _():
            acc[half] += part

    def normed_rope(vec, gain):
        mean = jnp.mean(vec * vec, axis=-1, keepdims=True)
        vec = vec * lax.rsqrt(mean + EPS) * gain
        return (vec * cos_ref[...] + pltpu.roll(vec, HEAD // 2, 1) * sin_ref[...]).astype(BF)

    def halo_copy(half, ahead_by):
        heads = pl.ds(half * 2, 2)
        return pltpu.make_async_remote_copy(
            src_ref=kv.at[:, heads, pl.ds(2 * TOK, TOK)],
            dst_ref=kv.at[:, heads, pl.ds((2 - ahead_by) * TOK, TOK)],
            send_sem=halo_send, recv_sem=halo_recv.at[ahead_by - 1, half],
            device_id=ahead[ahead_by - 1], device_id_type=MESH,
        )

    def kv_body(j, carry):
        half, kk = j // NK, j % NK
        project(0, half, kk, kk == 0)

        @pl.when(kk == NK - 1)
        def _():
            for h in range(2):
                kv[0, half * 2 + h, pl.ds(2 * TOK, TOK)] = normed_rope(
                    acc[half, :, h * HEAD : (h + 1) * HEAD], kg_ref[...]
                )
                kv[1, half * 2 + h, pl.ds(2 * TOK, TOK)] = acc[
                    half, :, (2 + h) * HEAD : (3 + h) * HEAD
                ].astype(BF)

        step = pick(j, KV_STEPS)

        @pl.when(step > 0)
        def _():
            comm_step(step)

        return carry

    def step_body(g, carry):
        comm_step(g)

        @pl.when(g == HALO_AT)
        def _():
            for half in range(2):
                halo_copy(half, 1).start()
                halo_copy(half, 2).start()

        return carry

    lax.fori_loop(0, 2 * NK, kv_body, 0)
    lax.fori_loop(KV_END, 28, step_body, 0)
    await_partner(1, 0, 14)

    def q_body(j, carry):
        mine = (j < 4) | ((j >= 6) & (j < 9))
        half = jnp.where(mine, xh, 1 - xh)
        p = pick(j, (0, 1, 2, 3, 0, 1, 4, 5, 6, 2, 3, 4, 5, 6))
        order = jnp.where(mine, pick(z * NK + p, Q_ORDER), pick(z * NK + p, Q_OTHER))

        @pl.when(j == 6)
        def _():
            lax.fori_loop(28, 30, step_body, 0)
            await_partner(1, 1, 2)

        project(1, half, order, p == 0)

        @pl.when(p == NK - 1)
        def _():
            for h in range(4):
                q[half * 2 + h // 2, h % 2] = normed_rope(
                    acc[half, :, h * HEAD : (h + 1) * HEAD], qg_ref[...]
                )

        step = pick(j, Q_STEPS)

        @pl.when(step > 0)
        def _():
            comm_step(step)

        return carry

    lax.fori_loop(0, 2 * NK, q_body, 0)
    lax.fori_loop(34, ATT_START, step_body, 0)
    for half in range(2):
        halo_copy(half, 1).wait_recv()
        halo_copy(half, 2).wait_recv()

    def attend(rel, qc, kvh):
        start = pl.multiple_of(qc * 128, 128)
        queries = q[kvh, :, pl.ds(start, 128), :].reshape(256, HEAD)
        keys = kv[0, kvh, pl.ds(start, 1152), :]
        values = kv[1, kvh, pl.ds(start, 1152), :]
        scores = lax.dot_general(
            queries, keys, (((1,), (1,)), ((), ())), preferred_element_type=F32
        )
        scores = scores.reshape(2, 128, 1152) * (SCALE * LOG2E) + bias[qc][None]
        expo = jnp.exp2(scores - jnp.max(scores, axis=-1, keepdims=True))
        total = jnp.sum(expo, axis=-1, keepdims=True).reshape(256, 1)
        weights = expo.astype(BF).reshape(256, 1152)
        mixed = jnp.dot(weights, values, preferred_element_type=F32)
        mixed = (mixed * (1.0 / total)).astype(BF)
        rows = pl.ds(pl.multiple_of(rel * 128, 128), 128)
        for h in range(2):
            lanes = pl.ds(pl.multiple_of((kvh % 2) * 256 + h * 128, 128), 128)
            att[kvh // 2, rows, lanes] = mixed[h * 128 : (h + 1) * 128]

    def attend_step(it):
        rel, pair = it // 2, it % 2
        qc = (y + pick(rel, (2, 0, 1, 3))) % 4
        attend(rel, qc, pair * 2)
        attend(rel, qc, pair * 2 + 1)

    def attend_body(it, carry):
        attend_step(it)
        lax.fori_loop(ATT_START + ATT_EACH * it, ATT_START + ATT_EACH * (it + 1), step_body, 0)
        return carry

    lax.fori_loop(0, 4, attend_body, 0)
    def drain(s):
        sent = w.at[s, 0, pl.ds(0, 10 * PIECE)]
        pltpu.make_async_copy(sent, sent, ici_send.at[s]).wait()
        pltpu.make_async_copy(w.at[s, 0], w.at[s, 0], part_send.at[s]).wait()

        def drain_body(k, carry):
            up, down = passes_on(s, k)

            @pl.when(up | down)
            def _():
                one = w.at[s, 0, pl.ds(0, PIECE)]
                pltpu.make_async_copy(one, one, pass_send.at[s, k]).wait()

            return carry

        lax.fori_loop(0, NSTEP, drain_body, 0)

    drain(0)

    def tile_of(n):
        u, mine = n // 2, n % 2 == 0
        by_x = jnp.where(mine, c, 1 - c) == 0
        other = jnp.where(by_x, pick(u, (1, 0, 1, 1, 0, 0, 1, 0)), pick(u, (1, 1, 1, 0, 0, 1, 0, 0)))
        dz = jnp.where(by_x, pick(u, (0, 0, 3, 1, 3, 1, 2, 2)), pick(u, (0, 3, 1, 0, 3, 2, 1, 2)))
        core = jnp.where(mine, c, 1 - c)
        return ((z + dz) % 4) * 4 + ((xl + other) % 2) * 2 + core

    def tile_rows(n):
        return pl.ds(pl.multiple_of(tile_of(n) * PIECE, 16), PIECE)

    def relay_copy(n, device):
        rows = tile_rows(n)
        return pltpu.make_async_remote_copy(
            src_ref=w.at[0, 0, rows, pl.ds(0, 128)], dst_ref=relay.at[rows],
            send_sem=rs_send, recv_sem=relay_recv.at[n], device_id=device, device_id_type=MESH,
        )

    def sum_copy(n, lane, side, device):
        rows = tile_rows(n)
        return pltpu.make_async_remote_copy(
            src_ref=w.at[0, 1, rows, pl.ds(lane, 128)], dst_ref=rbuf.at[side, rows],
            send_sem=rs_send, recv_sem=rs_recv.at[side, n], device_id=device, device_id_type=MESH,
        )

    def product(n, base):
        rows = tile_rows(n)
        dims = (((1,), (1,)), ((), ()))
        tokens = slice(base, base + 256)
        part = lax.dot_general(w[2, 0, rows, :], att[0, tokens], dims, preferred_element_type=F32)
        return part + lax.dot_general(
            w[2, 1, rows, :], att[1, tokens], dims, preferred_element_type=F32
        )

    def first_pass(n):
        u = n // 2

        @pl.when(n % 2 == 1)
        def _():
            by_x = c == 1
            one = jnp.where(by_x, pick(u, (0, 15, 5, 6, 2, 3, 10, 9)), pick(u, (2, 5, 7, 15, 0, 11, 1, 4)))
            two = jnp.where(by_x, pick(u, (1, 4, 7, 8, 11, 12, 13, 14)), pick(u, (3, 6, 8, 9, 10, 12, 13, 14)))
            await_partner(2, one, 1)
            await_partner(2, two, 1)

        w[0, 0, tile_rows(n), pl.ds(0, 256)] = product(n, 0).astype(BF)

        @pl.when(n % 2 == 0)
        def _():
            relay_copy(n, yp).start()

        @pl.when(n % 2 == 1)
        def _():
            relay_copy(n, ym).start()

        @pl.when((n < 8) & (n % 2 == 1))
        def _():
            attend_step(4 + n // 2)

    def second_pass(n):
        rows = tile_rows(n)
        relay_copy(n, yp).wait_recv()
        part = product(n, 256)
        term = relay[rows].astype(F32)
        even = n % 2 == 0
        w[0, 1, rows, pl.ds(0, 128)] = (part[:, :128] + jnp.where(even, term, 0.0)).astype(BF)
        w[0, 1, rows, pl.ds(128, 128)] = (part[:, 128:] + jnp.where(even, 0.0, term)).astype(BF)
        sum_copy(n, 0, 0, yp).start()
        sum_copy(n, 128, 1, ym).start()

    def take_sum(m):
        rows = tile_rows(m)
        sum_copy(m, 0, 0, yp).wait_recv()
        sum_copy(m, 128, 1, ym).wait_recv()
        value = (
            w[0, 0, rows, pl.ds(128, 128)].astype(F32)
            + rbuf[0, rows].astype(F32)
            + rbuf[1, rows].astype(F32)
        )
        padded = jnp.concatenate([value, jnp.zeros((176, 128), F32)], axis=0)
        proj[tile_of(m)] = pltpu.roll(padded.T, (tile_of(m) * PIECE) % 128, 1)
        squares[...] += jnp.sum(value * value, axis=0, keepdims=True)

    def out_body(i, carry):
        pair = (i - NT) // 2
        early = i < NT
        first = (early & (i < 8)) | among(pair, (0, 1, 3, 5))
        late = 2 * pick(pair, (4, 5, 4, 6, 5, 7, 6, 7)) + i % 2
        n = jnp.where(early, i % 8, late)
        step = pick(i, OUT_STEPS)

        @pl.when(step > 0)
        def _():
            comm_step(step)

        @pl.when((i < 2 * NT) & first)
        def _():
            first_pass(n)

        @pl.when((i < 2 * NT) & jnp.logical_not(first))
        def _():
            second_pass(n)

        @pl.when(i >= SUM_AT)
        def _():
            take_sum(i - SUM_AT)

        return carry

    squares[...] = jnp.zeros((1, 128), F32)
    lax.fori_loop(0, SUM_AT + NT, out_body, 0)
    scale = lax.rsqrt(squares[...] * (1.0 / D) + EPS)
    scale = jnp.broadcast_to(scale, (128, 128)).T[:, 0:1]
    post = pg_ref[...].reshape(1, D)
    for lane in range(0, D, 128):
        value = 0.0
        for t in range(lane // PIECE, (lane + 127) // PIECE + 1):
            at = lane - t * PIECE // 128 * 128
            value += proj[t, :, at : at + 128]
        cols = slice(lane, lane + 128)
        out_ref[:, cols] = (
            hid_ref[:, cols].astype(F32) + value * scale * post[:, cols]
        ).astype(BF)

    drain(1)
    drain(2)
    halo = kv.at[:, :, pl.ds(0, 2 * TOK)]
    pltpu.make_async_copy(halo, halo, halo_send).wait()
    summed = act.at[pl.ds(0, 3)]
    pltpu.make_async_copy(summed, summed, rs_send).wait()
    pltpu.make_async_copy(summed, summed, act_send).wait()


def per_device(
    hidden_in, in_gain, query_weight, key_weight, value_weight, out_weight, q_gain, k_gain, post_gain
):
    ctx, tp = lax.axis_index("ctx"), lax.axis_index("tp")
    block = ctx * 2 + tp // 4
    positions = block * TOK + jnp.arange(TOK, dtype=jnp.int32)
    frequency = 10000.0 ** (-(jnp.arange(HEAD // 2, dtype=F32) * 2.0 / HEAD))
    angles = positions.astype(F32)[:, None] * frequency[None, :]
    cosine, sine = jnp.cos(angles), jnp.sin(angles)
    cos_table = jnp.concatenate([cosine, cosine], axis=-1)
    sin_table = jnp.concatenate([-sine, sine], axis=-1)
    vmem, hbm = pl.BlockSpec(memory_space=pltpu.VMEM), pl.BlockSpec(memory_space=pl.ANY)
    dma = pltpu.SemaphoreType.DMA
    return pl.pallas_call(
        kernel,
        out_shape=jax.ShapeDtypeStruct((128, D), BF),
        in_specs=[vmem, vmem, hbm, hbm, hbm, hbm, vmem, vmem, vmem, vmem, vmem],
        out_specs=vmem,
        scratch_shapes=[
            pltpu.VMEM((3, 2, D, 512), BF),
            pltpu.VMEM((4, 128, D), BF),
            pltpu.VMEM((2, 4, 3 * TOK, HEAD), BF),
            pltpu.VMEM((4, 2, TOK, HEAD), BF),
            pltpu.VMEM((2, TOK, 512), BF),
            pltpu.VMEM((2, TOK, 512), F32),
            pltpu.VMEM((4, 128, 1152), F32),
            pltpu.VMEM((D, 128), BF),
            pltpu.VMEM((2, D, 128), BF),
            pltpu.VMEM((NT, 128, 512), F32),
            pltpu.VMEM((1, 128), F32),
            dma((4,)), dma((3, NSTEP)), dma((3, NSTEP + 1)), dma((3,)), dma((3, NSTEP)), dma((3,)),
            dma((6,)), dma, dma((2, 2)), dma, dma((NT,)), dma((2, NT)), dma,
        ],
        compiler_params=pltpu.CompilerParams(
            collective_id=0, has_side_effects=True, vmem_limit_bytes=67043328
        ),
    )(
        hidden_in,
        in_gain,
        query_weight,
        key_weight,
        value_weight,
        out_weight.T,
        cos_table,
        sin_table,
        q_gain.reshape(1, HEAD),
        k_gain.reshape(1, HEAD),
        post_gain,
    )


def solution(mesh):
    in_specs = (
        P(("ctx", "tp"), None), P(), P("ctx", "tp"), P("ctx", "tp"), P("ctx", "tp"), P("tp", "ctx"),
        P(), P(), P(),
    )
    return jax.shard_map(
        per_device, mesh=mesh, in_specs=in_specs, out_specs=P(("ctx", "tp"), None), check_vma=False
    )
```

```python
import functools

import jax
import jax.numpy as jnp
from jax import lax
from jax.experimental import pallas as pl
from jax.experimental.pallas import tpu as pltpu
from jax.sharding import PartitionSpec as P

WINDOW = 1024
SCALE = 168.0 ** (-0.5)
EPS = 1e-06
D = 5376
PIECE = 336
TOK = 512
HEAD = 128
KCH = 768
NK = D // KCH
NT = 16
SUM_AT = 20
MESH = pl.DeviceIdType.MESH
BF = jnp.bfloat16
F32 = jnp.float32

STEP_A = (-1, 1, 0, 0, 2, -1, -1, 1, 1, 0, -1, 2, 2, 1, 2)
STEP_B = (0, 0, -1, 1, 0, -1, 1, -1, 1, 2, 2, -1, 1, 2, 2)
NSTEP = 15
OUT_START = 12
KV_STEPS = (0, 0, 0, 19, 0, 0, 0, 20, 0, 0, 0, 21, 0, 0)
KV_END = 22
HALO_AT = 27
Q_STEPS = (0, 0, 0, 0, 0, 0, 0, 30, 0, 31, 0, 32, 0, 33)
ATT_START = 34
ATT_EACH = 1
OUT_STEPS = (0, 0, 38, 0, 0, 39, 0, 0, 0, 40, 0, 0, 0, 41, 0, 0, 0, 42, 0, 0, 43, 0, 0, 0, 44, 0)
Q_ORDER = (0, 2, 6, 1, 4, 3, 5, 2, 0, 4, 1, 3, 6, 5, 4, 2, 6, 3, 5, 0, 1, 6, 4, 0, 5, 2, 1, 3)
Q_OTHER = (0, 6, 1, 2, 3, 4, 5, 2, 0, 1, 3, 4, 5, 6, 4, 2, 3, 0, 1, 5, 6, 6, 4, 5, 0, 1, 2, 3)
LOG2E = 1.4426950408889634


def pick(k, values):
    out = jnp.int32(values[-1])
    for i in range(len(values) - 2, -1, -1):
        if values[i] != values[-1]:
            out = jnp.where(k == i, jnp.int32(values[i]), out)
    return out


def among(k, values):
    hit = k == values[0]
    for v in values[1:]:
        hit = hit | (k == v)
    return hit


def kernel(
    hid_ref, ing_ref, wq_ref, wk_ref, wv_ref, wo_ref, cos_ref, sin_ref, qg_ref, kg_ref, pg_ref,
    out_ref,
    w, act, kv, q, att, acc, bias, relay, rbuf, proj, squares,
    own_sem, ici_recv, part_recv, ici_send, pass_send, part_send,
    act_recv, act_send, halo_recv, halo_send, relay_recv, rs_recv, rs_send,
):
    ctx = lax.axis_index("ctx")
    tp = lax.axis_index("tp")
    z, xl, c = ctx // 4, (ctx // 2) % 2, ctx % 2
    xh, y = tp // 4, tp % 4
    x = xh * 2 + xl
    block = (z * 2 + xl) * 4 + c * 2 + xh

    def dev(dx, dz, core, dy):
        xx, zz, yy = (x + dx + 4) % 4, (z + dz + 4) % 4, (y + dy + 4) % 4
        return (zz * 4 + (xx % 2) * 2 + core, (xx // 2) * 4 + yy)

    def block_dev(b):
        return ((b // 8) * 4 + ((b // 4) % 2) * 2 + (b // 2) % 2, (b % 2) * 4 + y)

    yp, ym = dev(0, 0, c, 1), dev(0, 0, c, -1)
    partner = dev(0, 0, 1 - c, 0)
    ahead = [block_dev((block + 1) % 32), block_dev((block + 2) % 32)]
    behind = [block_dev((block + 31) % 32), block_dev((block + 30) % 32)]

    barrier = pltpu.get_barrier_semaphore()
    peers = [dev(1, 0, c, 0), dev(-1, 0, c, 0), dev(0, 1, c, 0), dev(0, -1, c, 0), yp, ym, partner]
    peers += ahead + behind
    for peer in peers:
        pl.semaphore_signal(barrier, inc=1, device_id=peer, device_id_type=MESH)

    own_rows = pl.ds(pl.multiple_of(ctx * PIECE, 16), PIECE)
    loads = [
        pltpu.make_async_copy(wk_ref, w.at[0, xh, own_rows, pl.ds(0, 256)], own_sem.at[0]),
        pltpu.make_async_copy(wv_ref, w.at[0, xh, own_rows, pl.ds(256, 256)], own_sem.at[1]),
        pltpu.make_async_copy(wq_ref, w.at[1, xh, own_rows], own_sem.at[2]),
        pltpu.make_async_copy(wo_ref, w.at[2, xh, own_rows], own_sem.at[3]),
    ]
    for load in loads:
        load.start()

    def x_first(s):
        return c == 0

    def axis_dev(s, first, sign):
        along_x = x_first(s) == first
        dx = jnp.where(along_x, sign, 0)
        dz = jnp.where(along_x, 0, sign)
        return dev(dx, dz, c, 0)

    def piece(s, da, db):
        fx = x_first(s)
        dx, dz = jnp.where(fx, da, db), jnp.where(fx, db, da)
        xx, zz = (x + dx + 4) % 4, (z + dz + 4) % 4
        row = pl.multiple_of((zz * 4 + (xx % 2) * 2 + c) * PIECE, 16)
        return w.at[s, xx // 2, pl.ds(row, PIECE)]

    def send(s, ref, device, at, sem):
        pltpu.make_async_remote_copy(
            src_ref=ref, dst_ref=ref, send_sem=sem, recv_sem=ici_recv.at[s, at],
            device_id=device, device_id_type=MESH,
        ).start()

    def send_partner(s, ref, k):
        late = jnp.where((s == 1) & (k > 12) & (k < NSTEP), 1, 0)
        pltpu.make_async_remote_copy(
            src_ref=ref, dst_ref=ref, send_sem=part_send.at[s],
            recv_sem=part_recv.at[s, jnp.where(s == 2, k, late)],
            device_id=partner, device_id_type=MESH,
        ).start()

    def start_own(s):
        ref = piece(s, 0, 0)
        send(s, ref, axis_dev(s, True, 1), 0, ici_send.at[s])
        send(s, ref, axis_dev(s, True, -1), 1, ici_send.at[s])
        send(s, ref, axis_dev(s, False, 1), 2, ici_send.at[s])
        send(s, ref, axis_dev(s, False, -1), 3, ici_send.at[s])
        send_partner(s, ref, NSTEP)

    def goes_plus(s, k):
        return jnp.where(k < 2, s % 2 == 0, among(k, (2, 3, 7, 8)))

    def passes_on(s, k):
        plus = goes_plus(s, k)
        up = among(k, (0, 2, 5, 7, 11)) & plus
        down = among(k, (1, 3, 6, 8, 12)) & jnp.logical_not(plus)
        return up, down

    def comm_step(g):
        s, k = g // NSTEP, g % NSTEP
        ref = piece(s, pick(k, STEP_A), pick(k, STEP_B))
        pltpu.make_async_copy(ref, ref, ici_recv.at[s, k]).wait()

        @pl.when(among(k, (0, 1, 4)))
        def _():
            at = pick(k, (5, 7, 0, 0, 11))
            send(s, ref, axis_dev(s, False, 1), at, ici_send.at[s])
            send(s, ref, axis_dev(s, False, -1), at + 1, ici_send.at[s])

        up, down = passes_on(s, k)

        @pl.when(up | down)
        def _():
            at = pick(k, (4, 4, 9, 9, 0, 10, 10, 13, 13, 0, 0, 14, 14))
            send(s, ref, axis_dev(s, k < 2, jnp.where(up, 1, -1)), at, pass_send.at[s, k])

        send_partner(s, ref, k)

        @pl.when(((k == 8) & (s == 0)) | ((k == OUT_START) & (s == 1)))
        def _():
            start_own(s + 1)

    def await_partner(s, at, count):
        ref = w.at[s, 0, pl.ds(0, count * PIECE)]
        pltpu.make_async_copy(ref, ref, part_recv.at[s, at]).wait()

    pl.semaphore_wait(barrier, len(peers))
    loads[0].wait()
    loads[1].wait()
    start_own(0)

    hid = hid_ref[...].astype(F32)
    mean = jnp.mean(hid * hid, axis=-1, keepdims=True)
    act[y] = (hid * lax.rsqrt(mean + EPS) * ing_ref[...].reshape(1, D)).astype(BF)
    loads[2].wait()
    loads[3].wait()

    def act_copy(owner, half, device, at):
        ref = act.at[owner, pl.ds(half * 64, 64)]
        return pltpu.make_async_remote_copy(
            src_ref=ref, dst_ref=ref, send_sem=act_send, recv_sem=act_recv.at[at],
            device_id=device, device_id_type=MESH,
        )

    act_copy(y, 0, yp, 0).start()
    act_copy(y, 1, ym, 3).start()
    act_copy(y, 1, yp, 1).start()
    act_copy(y, 0, ym, 2).start()
    before, after, across = (y + 3) % 4, (y + 1) % 4, (y + 2) % 4

    row = lax.broadcasted_iota(jnp.int32, (HEAD, 1152), 0)
    col = lax.broadcasted_iota(jnp.int32, (HEAD, 1152), 1)

    def mask_body(qc, carry):
        least = WINDOW - block * TOK - qc * 128
        allowed = (col > row) & (col <= row + WINDOW) & (col >= least)
        bias[qc] = jnp.where(allowed, 0.0, -1e30)
        return carry

    lax.fori_loop(0, 4, mask_body, 0)

    def stream_body(g, carry):
        comm_step(g)

        @pl.when(g == 8)
        def _():
            act_copy(before, 0, yp, 0).wait_recv()
            act_copy(before, 0, yp, 4).start()
            act_copy(after, 1, ym, 3).wait_recv()
            act_copy(after, 1, ym, 5).start()

        return carry

    lax.fori_loop(0, 19, stream_body, 0)
    act_copy(before, 1, yp, 1).wait_recv()
    act_copy(after, 0, ym, 2).wait_recv()
    act_copy(across, 0, yp, 4).wait_recv()
    act_copy(across, 1, ym, 5).wait_recv()
    await_partner(0, 0, 16)

    def project(s, half, kk, first):
        rows = pl.ds(pl.multiple_of(kk * KCH, KCH), KCH)
        left = act[:, :, rows].reshape(TOK, KCH)
        part = jnp.dot(left, w[s, half, rows, :], preferred_element_type=F32)

        @pl.when(first)
        def _():
            acc[half] = part

        @pl.when(jnp.logical_not(first))
        def _():
            acc[half] += part

    def normed_rope(vec, gain):
        mean = jnp.mean(vec * vec, axis=-1, keepdims=True)
        vec = vec * lax.rsqrt(mean + EPS) * gain
        return (vec * cos_ref[...] + pltpu.roll(vec, HEAD // 2, 1) * sin_ref[...]).astype(BF)

    def halo_copy(half, ahead_by):
        heads = pl.ds(half * 2, 2)
        return pltpu.make_async_remote_copy(
            src_ref=kv.at[:, heads, pl.ds(2 * TOK, TOK)],
            dst_ref=kv.at[:, heads, pl.ds((2 - ahead_by) * TOK, TOK)],
            send_sem=halo_send, recv_sem=halo_recv.at[ahead_by - 1, half],
            device_id=ahead[ahead_by - 1], device_id_type=MESH,
        )

    def kv_body(j, carry):
        half, kk = j // NK, j % NK
        project(0, half, kk, kk == 0)

        @pl.when(kk == NK - 1)
        def _():
            for h in range(2):
                kv[0, half * 2 + h, pl.ds(2 * TOK, TOK)] = normed_rope(
                    acc[half, :, h * HEAD : (h + 1) * HEAD], kg_ref[...]
                )
                kv[1, half * 2 + h, pl.ds(2 * TOK, TOK)] = acc[
                    half, :, (2 + h) * HEAD : (3 + h) * HEAD
                ].astype(BF)

        step = pick(j, KV_STEPS)

        @pl.when(step > 0)
        def _():
            comm_step(step)

        return carry

    def step_body(g, carry):
        comm_step(g)

        @pl.when(g == HALO_AT)
        def _():
            near = (c == 1) & (xh == 0)

            @pl.when(near)
            def _():
                for half in range(2):
                    halo_copy(half, 2).start()

            for half in range(2):
                halo_copy(half, 1).start()

            @pl.when(jnp.logical_not(near))
            def _():
                for half in range(2):
                    halo_copy(half, 2).start()

        return carry

    lax.fori_loop(0, 2 * NK, kv_body, 0)
    lax.fori_loop(KV_END, 28, step_body, 0)
    await_partner(1, 0, 14)

    def q_body(j, carry):
        mine = (j < 4) | ((j >= 6) & (j < 9))
        half = jnp.where(mine, xh, 1 - xh)
        p = pick(j, (0, 1, 2, 3, 0, 1, 4, 5, 6, 2, 3, 4, 5, 6))
        order = jnp.where(mine, pick(z * NK + p, Q_ORDER), pick(z * NK + p, Q_OTHER))

        @pl.when(j == 6)
        def _():
            lax.fori_loop(28, 30, step_body, 0)
            await_partner(1, 1, 2)

        project(1, half, order, p == 0)

        @pl.when(p == NK - 1)
        def _():
            for h in range(4):
                q[half * 2 + h // 2, h % 2] = normed_rope(
                    acc[half, :, h * HEAD : (h + 1) * HEAD], qg_ref[...]
                )

        step = pick(j, Q_STEPS)

        @pl.when(step > 0)
        def _():
            comm_step(step)

        return carry

    lax.fori_loop(0, 2 * NK, q_body, 0)
    lax.fori_loop(34, ATT_START, step_body, 0)
    for half in range(2):
        halo_copy(half, 1).wait_recv()
        halo_copy(half, 2).wait_recv()

    def attend(rel, qc, kvh):
        start = pl.multiple_of(qc * 128, 128)
        queries = q[kvh, :, pl.ds(start, 128), :].reshape(256, HEAD)
        keys = kv[0, kvh, pl.ds(start, 1152), :]
        values = kv[1, kvh, pl.ds(start, 1152), :]
        scores = lax.dot_general(
            queries, keys, (((1,), (1,)), ((), ())), preferred_element_type=F32
        )
        scores = scores.reshape(2, 128, 1152) * (SCALE * LOG2E) + bias[qc][None]
        expo = jnp.exp2(scores - jnp.max(scores, axis=-1, keepdims=True))
        total = jnp.sum(expo, axis=-1, keepdims=True).reshape(256, 1)
        weights = expo.astype(BF).reshape(256, 1152)
        mixed = jnp.dot(weights, values, preferred_element_type=F32)
        mixed = (mixed * (1.0 / total)).astype(BF)
        rows = pl.ds(pl.multiple_of(rel * 128, 128), 128)
        for h in range(2):
            lanes = pl.ds(pl.multiple_of((kvh % 2) * 256 + h * 128, 128), 128)
            att[kvh // 2, rows, lanes] = mixed[h * 128 : (h + 1) * 128]

    def attend_step(it):
        rel, pair = it // 2, it % 2
        qc = (y + pick(rel, (2, 0, 1, 3))) % 4
        attend(rel, qc, pair * 2)
        attend(rel, qc, pair * 2 + 1)

    def attend_body(it, carry):
        attend_step(it)
        lax.fori_loop(ATT_START + ATT_EACH * it, ATT_START + ATT_EACH * (it + 1), step_body, 0)
        return carry

    lax.fori_loop(0, 4, attend_body, 0)
    def drain(s):
        sent = w.at[s, 0, pl.ds(0, 10 * PIECE)]
        pltpu.make_async_copy(sent, sent, ici_send.at[s]).wait()
        pltpu.make_async_copy(w.at[s, 0], w.at[s, 0], part_send.at[s]).wait()

        def drain_body(k, carry):
            up, down = passes_on(s, k)

            @pl.when(up | down)
            def _():
                one = w.at[s, 0, pl.ds(0, PIECE)]
                pltpu.make_async_copy(one, one, pass_send.at[s, k]).wait()

            return carry

        lax.fori_loop(0, NSTEP, drain_body, 0)

    drain(0)

    def tile_of(n):
        u, mine = n // 2, n % 2 == 0
        by_x = jnp.where(mine, c, 1 - c) == 0
        other = jnp.where(by_x, pick(u, (1, 0, 1, 1, 0, 0, 1, 0)), pick(u, (1, 1, 1, 0, 0, 1, 0, 0)))
        dz = jnp.where(by_x, pick(u, (0, 0, 3, 1, 3, 1, 2, 2)), pick(u, (0, 3, 1, 0, 3, 2, 1, 2)))
        core = jnp.where(mine, c, 1 - c)
        return ((z + dz) % 4) * 4 + ((xl + other) % 2) * 2 + core

    def tile_rows(n):
        return pl.ds(pl.multiple_of(tile_of(n) * PIECE, 16), PIECE)

    def relay_copy(n, device):
        rows = tile_rows(n)
        return pltpu.make_async_remote_copy(
            src_ref=w.at[0, 0, rows, pl.ds(0, 128)], dst_ref=relay.at[rows],
            send_sem=rs_send, recv_sem=relay_recv.at[n], device_id=device, device_id_type=MESH,
        )

    def sum_copy(n, lane, side, device):
        rows = tile_rows(n)
        return pltpu.make_async_remote_copy(
            src_ref=w.at[0, 1, rows, pl.ds(lane, 128)], dst_ref=rbuf.at[side, rows],
            send_sem=rs_send, recv_sem=rs_recv.at[side, n], device_id=device, device_id_type=MESH,
        )

    def product(n, base):
        rows = tile_rows(n)
        dims = (((1,), (1,)), ((), ()))
        tokens = slice(base, base + 256)
        part = lax.dot_general(w[2, 0, rows, :], att[0, tokens], dims, preferred_element_type=F32)
        return part + lax.dot_general(
            w[2, 1, rows, :], att[1, tokens], dims, preferred_element_type=F32
        )

    def first_pass(n):
        u = n // 2

        @pl.when(n % 2 == 1)
        def _():
            by_x = c == 1
            one = jnp.where(by_x, pick(u, (0, 15, 5, 6, 2, 3, 10, 9)), pick(u, (2, 5, 7, 15, 0, 11, 1, 4)))
            two = jnp.where(by_x, pick(u, (1, 4, 7, 8, 11, 12, 13, 14)), pick(u, (3, 6, 8, 9, 10, 12, 13, 14)))
            await_partner(2, one, 1)
            await_partner(2, two, 1)

        w[0, 0, tile_rows(n), pl.ds(0, 256)] = product(n, 0).astype(BF)

        @pl.when(n % 2 == 0)
        def _():
            relay_copy(n, yp).start()

        @pl.when(n % 2 == 1)
        def _():
            relay_copy(n, ym).start()

        @pl.when((n < 8) & (n % 2 == 1))
        def _():
            attend_step(4 + n // 2)

    def second_pass(n):
        rows = tile_rows(n)
        relay_copy(n, yp).wait_recv()
        part = product(n, 256)
        term = relay[rows].astype(F32)
        even = n % 2 == 0
        w[0, 1, rows, pl.ds(0, 128)] = (part[:, :128] + jnp.where(even, term, 0.0)).astype(BF)
        w[0, 1, rows, pl.ds(128, 128)] = (part[:, 128:] + jnp.where(even, 0.0, term)).astype(BF)
        sum_copy(n, 0, 0, yp).start()
        sum_copy(n, 128, 1, ym).start()

    def take_sum(m):
        rows = tile_rows(m)
        sum_copy(m, 0, 0, yp).wait_recv()
        sum_copy(m, 128, 1, ym).wait_recv()
        value = (
            w[0, 0, rows, pl.ds(128, 128)].astype(F32)
            + rbuf[0, rows].astype(F32)
            + rbuf[1, rows].astype(F32)
        )
        padded = jnp.concatenate([value, jnp.zeros((176, 128), F32)], axis=0)
        proj[tile_of(m)] = pltpu.roll(padded.T, (tile_of(m) * PIECE) % 128, 1)
        squares[...] += jnp.sum(value * value, axis=0, keepdims=True)

    def out_body(i, carry):
        pair = (i - NT) // 2
        early = i < NT
        first = (early & (i < 8)) | among(pair, (0, 1, 3, 5))
        late = 2 * pick(pair, (4, 5, 4, 6, 5, 7, 6, 7)) + i % 2
        n = jnp.where(early, i % 8, late)
        step = pick(i, OUT_STEPS)

        @pl.when(step > 0)
        def _():
            comm_step(step)

        @pl.when((i < 2 * NT) & first)
        def _():
            first_pass(n)

        @pl.when((i < 2 * NT) & jnp.logical_not(first))
        def _():
            second_pass(n)

        @pl.when(i >= SUM_AT)
        def _():
            take_sum(i - SUM_AT)

        return carry

    squares[...] = jnp.zeros((1, 128), F32)
    lax.fori_loop(0, SUM_AT + NT, out_body, 0)
    scale = lax.rsqrt(squares[...] * (1.0 / D) + EPS)
    scale = jnp.broadcast_to(scale, (128, 128)).T[:, 0:1]
    post = pg_ref[...].reshape(1, D)
    for lane in range(0, D, 128):
        value = 0.0
        for t in range(lane // PIECE, (lane + 127) // PIECE + 1):
            at = lane - t * PIECE // 128 * 128
            value += proj[t, :, at : at + 128]
        cols = slice(lane, lane + 128)
        out_ref[:, cols] = (
            hid_ref[:, cols].astype(F32) + value * scale * post[:, cols]
        ).astype(BF)

    drain(1)
    drain(2)
    halo = kv.at[:, :, pl.ds(0, 2 * TOK)]
    pltpu.make_async_copy(halo, halo, halo_send).wait()
    summed = act.at[pl.ds(0, 3)]
    pltpu.make_async_copy(summed, summed, rs_send).wait()
    pltpu.make_async_copy(summed, summed, act_send).wait()


def per_device(
    hidden_in, in_gain, query_weight, key_weight, value_weight, out_weight, q_gain, k_gain, post_gain
):
    ctx, tp = lax.axis_index("ctx"), lax.axis_index("tp")
    block = ctx * 2 + tp // 4
    positions = block * TOK + jnp.arange(TOK, dtype=jnp.int32)
    lane = jnp.arange(HEAD, dtype=jnp.int32)
    frequency = 10000.0 ** (-((lane % (HEAD // 2)).astype(F32) * 2.0 / HEAD))
    angles = positions.astype(F32)[:, None] * frequency[None, :]
    cos_table = jnp.cos(angles)
    sin_table = jnp.sin(angles) * jnp.where(lane < HEAD // 2, -1.0, 1.0)[None, :]
    vmem, hbm = pl.BlockSpec(memory_space=pltpu.VMEM), pl.BlockSpec(memory_space=pl.ANY)
    dma = pltpu.SemaphoreType.DMA
    return pl.pallas_call(
        kernel,
        out_shape=jax.ShapeDtypeStruct((128, D), BF),
        in_specs=[vmem, vmem, hbm, hbm, hbm, hbm, vmem, vmem, vmem, vmem, vmem],
        out_specs=vmem,
        scratch_shapes=[
            pltpu.VMEM((3, 2, D, 512), BF),
            pltpu.VMEM((4, 128, D), BF),
            pltpu.VMEM((2, 4, 3 * TOK, HEAD), BF),
            pltpu.VMEM((4, 2, TOK, HEAD), BF),
            pltpu.VMEM((2, TOK, 512), BF),
            pltpu.VMEM((2, TOK, 512), F32),
            pltpu.VMEM((4, 128, 1152), F32),
            pltpu.VMEM((D, 128), BF),
            pltpu.VMEM((2, D, 128), BF),
            pltpu.VMEM((NT, 128, 512), F32),
            pltpu.VMEM((1, 128), F32),
            dma((4,)), dma((3, NSTEP)), dma((3, NSTEP + 1)), dma((3,)), dma((3, NSTEP)), dma((3,)),
            dma((6,)), dma, dma((2, 2)), dma, dma((NT,)), dma((2, NT)), dma,
        ],
        compiler_params=pltpu.CompilerParams(
            collective_id=0, has_side_effects=True, vmem_limit_bytes=67043328
        ),
    )(
        hidden_in,
        in_gain,
        query_weight,
        key_weight,
        value_weight,
        out_weight.T,
        cos_table,
        sin_table,
        q_gain.reshape(1, HEAD),
        k_gain.reshape(1, HEAD),
        post_gain,
    )


def solution(mesh):
    in_specs = (
        P(("ctx", "tp"), None), P(), P("ctx", "tp"), P("ctx", "tp"), P("ctx", "tp"), P("tp", "ctx"),
        P(), P(), P(),
    )
    return jax.shard_map(
        per_device, mesh=mesh, in_specs=in_specs, out_specs=P(("ctx", "tp"), None), check_vma=False
    )
```
